32 devices in a mesh: rollout: 2 (over y), branch: 4 (over z), seq: 4 (over x, core).
Axes of the slice: x: 2, y: 2, z: 4, core: 2. Of those that a mesh axis runs over, the one named last changes fastest.
Arguments:
- queries: bfloat16 [8, 512, 4096], P(('rollout', 'branch'), 'seq'), parts along dimension 0, may hold values from -8 to 8
- keyvals: bfloat16 [8, 512, 2, 256], P(('rollout', 'branch'), 'seq'), parts along dimension 0, may hold values from -4 to 4
- residual: bfloat16 [8, 512, 4096], P(('rollout', 'branch'), 'seq'), parts along dimension 0, may hold values from -3 to 3
- read_list: int32 [8, 4, 3], P(('rollout', 'branch'), 'seq'), parts along dimension 0, may hold values from 0 to 3
- router: bfloat16 [4096, 8], replicated, may hold values from -0.09375 to 0.09375
- expert_ids: int32 [8, 512, 2], P(('rollout', 'branch'), 'seq'), parts along dimension 0, may hold values from 0 to 7, all different within a row; in each aligned block of 128 rows (0 to 127, 128 to 255, ..., all dimensions but the last counted through in order) at most 48 rows name the same one
- w_gate_up: bfloat16 [16, 4096, 2, 384], P(('branch', 'seq')), may hold values from -0.09375 to 0.09375
- w_down: bfloat16 [16, 384, 4096], P(('branch', 'seq')), may hold values from -0.21875 to 0.21875
Outputs:
- mixed: bfloat16 [8, 512, 4096], P(('rollout', 'branch'), 'seq'), parts along dimension 0
The draws below stay inside these ranges and needn't reach their ends.
There are 2 independent parts, one for each index of `rollout`. The reference program is written for one: setup_inputs(seed, part) draws one part's arguments, and reference() takes and returns one part's arrays. A program takes and returns all parts, laid end to end along the dimension named above; an argument that names none is the same for every part. Nothing has to cross between parts.
Inputs may be any that keep to these rules, and one draw needn't show every extreme that they name: read_list[c, s, o] is the block of branch c that query block s of branch (c + o + 1) mod 4 reads. `expert_ids`: each token names 2 different experts; of the 128 tokens of one device at most 48 name one expert, and in every draw some expert is named by exactly 48 tokens of some device.
All inputs are finite; a program needn't handle non-finite values.
Results may differ from the reference program's by a relative error of at most 0.0062.
Values may be sent and summed in bfloat16 or wider, within the bound.
A program may use at most 192 MiB of HBM per device.

```python
import math
import jax
import jax.numpy as jnp
import numpy as np
from jax import lax

D = 4096
HEAD_SIZE = 128
QUERY_HEADS = 32
KEY_VALUE_HEADS = 2
FF = 768
TOP = 2
TOK_DEV = 128
SIBLING_COUNT = 4
NBLK = 4
SUFFIX_LENGTH = 512
EXPERTS = 8
CAP = 48
N_BRANCH = 4
N_SEQ = 4


def draw_queries(key, part):
    complete_shape = (SIBLING_COUNT, SUFFIX_LENGTH, QUERY_HEADS * HEAD_SIZE)
    drawn = jnp.clip(2.0 * jax.random.normal(jax.random.fold_in(key, 11), complete_shape, jnp.float32), -8.0, 8.0)
    return drawn.astype(jnp.bfloat16)


def draw_keyvals(key, part):
    complete_shape = (SIBLING_COUNT, SUFFIX_LENGTH, 2, KEY_VALUE_HEADS * HEAD_SIZE)
    drawn = jnp.clip(jax.random.normal(jax.random.fold_in(key, 21), complete_shape, jnp.float32), -4.0, 4.0)
    return drawn.astype(jnp.bfloat16)


def plant(values, stream_key, least, top_value):
    longest = values.shape.index(max(values.shape))
    spots = []
    for shift in (0, 1):
        where = [jax.random.randint(jax.random.fold_in(stream_key, axis), (), 0, length) for axis, length in enumerate(values.shape)]
        where[longest] = (where[longest] + shift) % values.shape[longest]
        spots.append(tuple(where))
    return values.at[spots[0]].set(least).at[spots[1]].set(top_value)


def levels(stream_key, extent, shards, smallest, top_value):
    gain = 1.0
    for position, parts in shards:
        heights = jax.random.uniform(jax.random.fold_in(jax.random.fold_in(stream_key, 6), position), (parts,), jnp.float32, smallest / len(shards), top_value / len(shards))
        gain = gain * jnp.repeat(jnp.exp(heights), extent[position] // parts).reshape((-1,) + (1,) * (len(extent) - 1 - position))
    return gain


def deal_out(own_key, own, number, rows, amount, top, limit, lean):
    sequence = jax.random.permutation(own_key, amount)
    crowded, common = shares(amount, rows * top, limit, lean, True), shares(amount, rows * top, limit, lean, False)
    places = jnp.arange(amount)

    def named(tallies, turn):
        used = int((tallies > 0).sum())
        fixed = max(1, used // 4)
        moved = fixed + (places - fixed + turn * (used - fixed)) % max(1, amount - fixed)
        return jnp.zeros((amount,), jnp.int32).at[sequence[jnp.where(places < fixed, places, moved)]].set(jnp.asarray(tallies, jnp.int32))

    tallies = jnp.where(number % 4 == 0, named(crowded, number // 4), named(common, number - number // 4 - 1))
    mixed = jax.random.permutation(jax.random.fold_in(own, 3), amount)
    donor, taker = mixed[0:amount // 2 * 2:2], mixed[1:amount // 2 * 2:2]
    margin = jnp.minimum(tallies[donor] - 1, limit - tallies[taker]) // 2
    margin = jnp.where((donor == sequence[0]) | (taker == sequence[0]) | (tallies[taker] == 0), 0, jnp.maximum(margin, 0))
    moved = jax.random.randint(jax.random.fold_in(own, 4), (amount // 2,), 0, 1 << 20) % (margin + 1)
    tallies = tallies.at[donor].add(-moved).at[taker].add(moved)
    members = jnp.searchsorted(jnp.cumsum(tallies), jnp.arange(rows * top), side="right").astype(jnp.int32)
    grid = members.reshape(top, rows).T
    grid = grid[jax.random.permutation(jax.random.fold_in(own, 1), rows)]
    turn = jax.random.randint(jax.random.fold_in(own, 2), (rows, 1), 0, top)
    return jnp.take_along_axis(grid, (jnp.arange(top)[None, :] + turn) % top, axis=1)


def shares(count, total, bound, skew, full):
    weights = [(1 << 20) // math.isqrt(standing ** skew) + 1 for standing in range(1, count + 1)]
    largest = bound if full else min(bound, max(-(-total // count), total * weights[0] // sum(weights)))
    least = 1 if total - largest >= count - 1 else 0
    given, surplus = [largest] + [least] * (count - 1), total - largest - least * (count - 1)
    while surplus > 0:
        free = [i for i in range(1, count) if given[i] < largest] or [i for i in range(1, count) if given[i] < bound]
        mass, budget = sum([weights[i] for i in free]), surplus
        for i in free:
            extra = min(bound - given[i], max(1, budget * weights[i] // mass), surplus)
            given[i] = given[i] + extra
            surplus = surplus - extra
    return np.array(given)


def bell_draw(key, shape, scale, reach, cuts=(), kind=jnp.bfloat16):
    entries = scale * jax.random.normal(key, shape, jnp.float32)
    if cuts:
        entries = entries * levels(key, shape, cuts, -0.22, 0.18)
    return jnp.clip(entries, -reach, reach).astype(kind)


def setup_inputs(seed: int = 0, part: int = 0) -> dict:
    key_of = jax.random.split(jax.random.key(seed), 9)
    part_splits = jax.random.split(jax.random.fold_in(key_of[8], part), 9)
    queries = draw_queries(jax.random.fold_in(jax.random.fold_in(key_of[8], part), 71), part)
    keyvals = draw_keyvals(jax.random.fold_in(jax.random.fold_in(key_of[8], part), 71), part)
    residual = bell_draw(part_splits[2], (SIBLING_COUNT, SUFFIX_LENGTH, D), 0.5, 3.0, ((0, 4), (1, 4)))
    read_list = plant(jax.random.randint(part_splits[3], (SIBLING_COUNT, NBLK, SIBLING_COUNT - 1), 0, NBLK), jax.random.fold_in(part_splits[3], 1), 0, NBLK - 1).astype(jnp.int32)
    router = bell_draw(key_of[4], (D, EXPERTS), D ** -0.5, 0.09375)
    expert_ids_keys = jax.random.split(jax.random.fold_in(part_splits[5], 1), SIBLING_COUNT * SUFFIX_LENGTH // TOK_DEV)
    expert_ids_turns = jax.random.permutation(jax.random.fold_in(part_splits[5], 3), SIBLING_COUNT * SUFFIX_LENGTH // TOK_DEV)
    expert_ids = jax.vmap(lambda own, number: deal_out(jax.random.fold_in(part_splits[5], 2), own, number, TOK_DEV, EXPERTS, TOP, CAP, 2))(expert_ids_keys, expert_ids_turns).reshape((SIBLING_COUNT, SUFFIX_LENGTH, TOP))
    w_gate_up = bell_draw(key_of[6], (2 * EXPERTS, D, 2, FF // 2), D ** -0.5, 0.09375, ((0, 16),))
    w_down = bell_draw(key_of[7], (2 * EXPERTS, FF // 2, D), FF ** -0.5, 0.21875, ((0, 16),))
    return {"queries": queries, "keyvals": keyvals, "residual": residual, "read_list": read_list, "router": router, "expert_ids": expert_ids, "w_gate_up": w_gate_up, "w_down": w_down}


def attend_block(q_rows, own_kv, sib_kv, block_index):
    block_len = q_rows.shape[0]
    length_own = own_kv.shape[0]
    positions = block_index * block_len + jnp.arange(block_len, dtype=jnp.int32)
    own_allowed = jnp.arange(length_own, dtype=jnp.int32)[None, :] <= positions[:, None]
    allowed = jnp.concatenate([own_allowed, jnp.ones((block_len, sib_kv.shape[0]), dtype=bool)], axis=1)
    key_rows = jnp.concatenate([own_kv[:, 0], sib_kv[:, 0]], axis=0).astype(jnp.float32)
    value_rows = jnp.concatenate([own_kv[:, 1], sib_kv[:, 1]], axis=0).astype(jnp.float32)
    group_count = QUERY_HEADS // KEY_VALUE_HEADS
    inv_scale = 1.0 / math.sqrt(HEAD_SIZE)
    pieces = []
    for head_key_value in range(KEY_VALUE_HEADS):
        key_head = key_rows[:, head_key_value * HEAD_SIZE:(head_key_value + 1) * HEAD_SIZE]
        value_head = value_rows[:, head_key_value * HEAD_SIZE:(head_key_value + 1) * HEAD_SIZE]
        query_head = q_rows[:, head_key_value * group_count * HEAD_SIZE:(head_key_value + 1) * group_count * HEAD_SIZE]
        query_head = query_head.reshape(block_len, group_count, HEAD_SIZE).astype(jnp.float32)
        scores = jnp.einsum('tgd,kd->gtk', query_head, key_head) * inv_scale
        scores = jnp.where(allowed[None], scores, -1e+30)
        row_max = lax.optimization_barrier(jnp.max(scores, axis=-1, keepdims=True))
        expterm = jnp.exp(scores - row_max)
        probs = (expterm / lax.optimization_barrier(jnp.sum(expterm, axis=-1, keepdims=True))).astype(jnp.bfloat16)
        mixture = jnp.einsum('gtk,kd->tgd', probs.astype(jnp.float32), value_head)
        pieces.append(mixture.reshape(block_len, group_count * HEAD_SIZE))
    return jnp.concatenate(pieces, axis=1).astype(jnp.bfloat16)

def reference(queries, keyvals, residual, read_list, router, expert_ids, w_gate_up, w_down):
    block_len = TOK_DEV
    kv_width = keyvals.shape[-1]
    blocks = keyvals.reshape(SIBLING_COUNT, NBLK, block_len, 2, kv_width)

    def one_block(block_item):
        branch = block_item // NBLK
        block_at = block_item % NBLK
        others = ((branch + 1 + jnp.arange(SIBLING_COUNT - 1, dtype=jnp.int32)) % SIBLING_COUNT).astype(jnp.int32)
        offset = ((branch - others - 1) % SIBLING_COUNT).astype(jnp.int32)
        chosen = read_list[others, block_at, offset].astype(jnp.int32)
        sibling = blocks[others, chosen].reshape((SIBLING_COUNT - 1) * block_len, 2, kv_width)
        own_kv = keyvals[branch]
        q_rows = lax.dynamic_slice_in_dim(queries[branch], (block_at * block_len).astype(jnp.int32), block_len, 0)
        return attend_block(q_rows, own_kv, sibling, block_at)
    context = lax.map(one_block, jnp.arange(SIBLING_COUNT * NBLK, dtype=jnp.int32))
    context = context.reshape(SIBLING_COUNT, SUFFIX_LENGTH, QUERY_HEADS * HEAD_SIZE)
    state = residual.astype(jnp.float32) + context.astype(jnp.float32)
    normed = (state * lax.rsqrt(lax.optimization_barrier(jnp.mean(state * state, axis=-1, keepdims=True)) + 1e-06)).astype(jnp.bfloat16)
    flat_rows = normed.reshape(-1, D)
    logits = jnp.dot(flat_rows, router, preferred_element_type=jnp.float32)
    routed = expert_ids.reshape(-1, TOP).astype(jnp.int32)
    chosen_logits = jnp.take_along_axis(logits, routed, axis=1)
    gate_mix = 1.0 / lax.optimization_barrier(jnp.sum(jnp.exp(chosen_logits[:, None, :] - chosen_logits[:, :, None]), axis=-1))
    flat_ids = routed.reshape(-1)
    rows_total = flat_ids.shape[0]
    most_rows = N_BRANCH * N_SEQ * CAP
    paired = w_gate_up.reshape(EXPERTS, 2, D, 2, FF // 2)
    down_pairs = w_down.reshape(EXPERTS, 2, FF // 2, D)

    def one_expert(expert, out_table):
        row_at = jnp.nonzero(flat_ids == expert, size=most_rows, fill_value=rows_total)[0].astype(jnp.int32)
        token_at = jnp.minimum(row_at, rows_total - 1) // TOP
        expert_rows = flat_rows[token_at]
        pair_now = paired[expert]
        gate_cols = jnp.concatenate([pair_now[0, :, 0], pair_now[1, :, 0]], axis=1)
        up_cols = jnp.concatenate([pair_now[0, :, 1], pair_now[1, :, 1]], axis=1)
        down_rows = jnp.concatenate([down_pairs[expert, 0], down_pairs[expert, 1]], axis=0)
        gate_val = jnp.dot(expert_rows, gate_cols, preferred_element_type=jnp.float32)
        up_val = jnp.dot(expert_rows, up_cols, preferred_element_type=jnp.float32)
        hidden_act = (jax.nn.silu(gate_val) * up_val).astype(jnp.bfloat16)
        outputs = jnp.dot(hidden_act, down_rows, preferred_element_type=jnp.float32).astype(jnp.bfloat16)
        return out_table.at[row_at].set(outputs, mode='drop')
    out_table = jnp.zeros((rows_total, D), jnp.bfloat16)
    out_table = lax.fori_loop(0, EXPERTS, one_expert, out_table)
    expert_out = out_table.reshape(-1, TOP, D)
    layer_out = state.reshape(-1, D)
    for slot_k in range(TOP):
        layer_out = layer_out + gate_mix[:, slot_k:slot_k + 1] * expert_out[:, slot_k].astype(jnp.float32)
    return layer_out.reshape(SIBLING_COUNT, SUFFIX_LENGTH, D).astype(jnp.bfloat16)
```

```python
import functools
import math

import jax
import jax.numpy as jnp
from jax import lax
from jax.experimental import pallas as pl
from jax.experimental.pallas import tpu as pltpu
from jax.sharding import PartitionSpec as P

HEAD_SIZE = 128
VMEM_LIMIT = 60 * 1024 * 1024
F32 = jnp.float32
BF16 = jnp.bfloat16
ANY = pl.BlockSpec(memory_space=pl.ANY)
VMEM = pl.BlockSpec(memory_space=pltpu.VMEM)
SMEM = pl.BlockSpec(memory_space=pltpu.SMEM)


def flipped(number, mask, count):
    value, bit = 0, 1
    while bit < count:
        value = value + ((number // bit + mask // bit) % 2) * bit
        bit *= 2
    return value


def kv_kernel(n_branch, n_seq, list_ref, kv_ref, own_ref, sib_ref, picked, s1, r1, s2, r2, lsem):
    branch = lax.axis_index("branch")
    seq = lax.axis_index("seq")
    barrier = pltpu.get_barrier_semaphore()
    for step in range(1, n_seq):
        pl.semaphore_signal(
            barrier, inc=1, device_id={"seq": (seq + step) % n_seq},
            device_id_type=pl.DeviceIdType.MESH,
        )
    for step in range(1, n_branch):
        pl.semaphore_signal(
            barrier, inc=1, device_id={"branch": (branch + step) % n_branch},
            device_id_type=pl.DeviceIdType.MESH,
        )
    pl.semaphore_wait(barrier, n_seq - 1 + n_branch - 1)
    mine = pltpu.make_async_copy(kv_ref, own_ref.at[seq], lsem)
    mine.start()
    first = []
    for step in range(1, n_seq):
        copy = pltpu.make_async_remote_copy(
            src_ref=kv_ref, dst_ref=own_ref.at[seq],
            send_sem=s1.at[step], recv_sem=r1.at[step],
            device_id={"seq": (seq + step) % n_seq}, device_id_type=pl.DeviceIdType.MESH,
        )
        copy.start()
        first.append(copy)
    mine.wait()
    for copy in first:
        copy.wait()
    second = []
    for offset in range(n_branch - 1):
        picked[offset] = own_ref[list_ref[offset]]
    for offset in range(n_branch - 1):
        copy = pltpu.make_async_remote_copy(
            src_ref=picked.at[offset], dst_ref=sib_ref.at[offset],
            send_sem=s2.at[offset], recv_sem=r2.at[offset],
            device_id={"branch": (branch + offset + 1) % n_branch},
            device_id_type=pl.DeviceIdType.MESH,
        )
        copy.start()
        second.append(copy)
    for copy in second:
        copy.wait()


def exchange_kv(kv, listed, n_branch, n_seq):
    rows, width = kv.shape
    return pl.pallas_call(
        functools.partial(kv_kernel, n_branch, n_seq),
        out_shape=(
            jax.ShapeDtypeStruct((n_seq, rows, width), BF16),
            jax.ShapeDtypeStruct((n_branch - 1, rows, width), BF16),
        ),
        in_specs=[SMEM, VMEM],
        out_specs=(VMEM, VMEM),
        scratch_shapes=[
            pltpu.VMEM((n_branch - 1, rows, width), BF16),
            pltpu.SemaphoreType.DMA((n_seq,)),
            pltpu.SemaphoreType.DMA((n_seq,)),
            pltpu.SemaphoreType.DMA((n_branch,)),
            pltpu.SemaphoreType.DMA((n_branch,)),
            pltpu.SemaphoreType.DMA,
        ],
        compiler_params=pltpu.CompilerParams(
            collective_id=0, has_side_effects=True, vmem_limit_bytes=VMEM_LIMIT
        ),
    )(listed, kv)


def attend_kernel(
    experts, cap, n_seq,
    q_ref, own_ref, sib_ref, res_ref, router_ref, ids_ref, idt_ref,
    send_ref, state_ref, gate_ref,
):
    seq = lax.axis_index("seq")
    me = (lax.axis_index("branch") * n_seq + seq) // 2
    rows, width = q_ref.shape
    kv_heads = own_ref.shape[1] // (2 * HEAD_SIZE)
    group = width // HEAD_SIZE // kv_heads
    together = 2
    own_len = own_ref.shape[0]
    scale = 1.0 / math.sqrt(HEAD_SIZE)
    nt = (((1,), (1,)), ((), ()))
    where = seq * rows + lax.broadcasted_iota(jnp.int32, (together * rows, own_len), 0) % rows
    bias = jnp.where(
        lax.broadcasted_iota(jnp.int32, (together * rows, own_len), 1) <= where, 0.0, -1e30
    )
    for head in range(kv_heads):
        kcol = slice(head * HEAD_SIZE, (head + 1) * HEAD_SIZE)
        vcol = slice((kv_heads + head) * HEAD_SIZE, (kv_heads + head + 1) * HEAD_SIZE)

        @pl.loop(0, group // together)
        def _(step):
            base = (head * group + step * together) * HEAD_SIZE
            cols = [
                pl.ds(pl.multiple_of(base + i * HEAD_SIZE, HEAD_SIZE), HEAD_SIZE)
                for i in range(together)
            ]
            q = jnp.concatenate([q_ref[:, c] for c in cols], axis=0)
            s_own = lax.dot_general(q, own_ref[:, kcol], nt, preferred_element_type=F32)
            s_sib = lax.dot_general(q, sib_ref[:, kcol], nt, preferred_element_type=F32)
            s_own = s_own * scale + bias
            s_sib = s_sib * scale
            top = jnp.maximum(
                jnp.max(s_own, axis=1, keepdims=True), jnp.max(s_sib, axis=1, keepdims=True)
            )
            p_own = jnp.exp(s_own - top)
            p_sib = jnp.exp(s_sib - top)
            total = jnp.sum(p_own, axis=1, keepdims=True) + jnp.sum(p_sib, axis=1, keepdims=True)
            mixed = jnp.dot(p_own.astype(BF16), own_ref[:, vcol], preferred_element_type=F32)
            mixed += jnp.dot(p_sib.astype(BF16), sib_ref[:, vcol], preferred_element_type=F32)
            mixed = (mixed / total).astype(BF16).astype(F32)
            for i, c in enumerate(cols):
                state_ref[:, c] = res_ref[:, c].astype(F32) + mixed[i * rows : (i + 1) * rows]

    state = state_ref[...]
    normed = (
        state * lax.rsqrt(jnp.mean(state * state, axis=1, keepdims=True) + 1e-06)
    ).astype(BF16)
    logits = lax.dot_general(normed, router_ref[...], nt, preferred_element_type=F32)

    top_count = ids_ref.shape[1]
    ids, idt = ids_ref[...], idt_ref[...]
    kinds = lax.broadcasted_iota(jnp.int32, (rows, experts), 1)
    kinds_t = lax.broadcasted_iota(jnp.int32, (experts, rows), 0)
    hot = [(ids[:, k : k + 1] == kinds).astype(F32) for k in range(top_count)]
    hot_t = [(idt[k : k + 1, :] == kinds_t).astype(F32) for k in range(top_count)]
    down = lax.broadcasted_iota(jnp.int32, (rows, rows), 0)
    along = lax.broadcasted_iota(jnp.int32, (rows, rows), 1)
    before = jnp.dot((along < down).astype(F32).astype(BF16), sum(hot).astype(BF16), preferred_element_type=F32)
    before_t = jnp.dot(sum(hot_t).astype(BF16), (down < along).astype(F32).astype(BF16), preferred_element_type=F32)
    dest, dest_t = [], []
    for k in range(top_count):
        slot = jnp.sum(before * hot[k], axis=1, keepdims=True).astype(jnp.int32)
        dest.append((ids[:, k : k + 1] ^ me) * cap + slot)
        slot_t = jnp.sum(before_t * hot_t[k], axis=0, keepdims=True).astype(jnp.int32)
        dest_t.append((idt[k : k + 1, :] ^ me) * cap + slot_t)
    chosen = [jnp.sum(logits * hot[k], axis=1, keepdims=True) for k in range(top_count)]
    gates = [1.0 / sum(jnp.exp(c - chosen[k]) for c in chosen) for k in range(top_count)]

    pair = 2 * cap
    places = lax.broadcasted_iota(jnp.int32, (rows, pair), 1)
    places_t = lax.broadcasted_iota(jnp.int32, (pair, rows), 0)
    for p in range(experts // 2):
        pick = sum((dest_t[k] - p * pair == places_t).astype(F32) for k in range(top_count))
        send_ref[p * pair : (p + 1) * pair, :] = jnp.dot(
            pick.astype(BF16), normed, preferred_element_type=F32
        ).astype(BF16)
        weight = sum(
            jnp.where(dest[k] - p * pair == places, gates[k], 0.0) for k in range(top_count)
        )
        high = weight.astype(BF16)
        gate_ref[p, 0] = high
        gate_ref[p, 1] = (weight - high.astype(F32)).astype(BF16)


def attend(q, own, sib, residual, router_t, ids, experts, cap, n_seq):
    rows, width = q.shape
    return pl.pallas_call(
        functools.partial(attend_kernel, experts, cap, n_seq),
        out_shape=(
            jax.ShapeDtypeStruct((experts * cap, width), BF16),
            jax.ShapeDtypeStruct((rows, width), F32),
            jax.ShapeDtypeStruct((experts // 2, 2, rows, 2 * cap), BF16),
        ),
        in_specs=[VMEM] * 7,
        out_specs=(VMEM, VMEM, VMEM),
        compiler_params=pltpu.CompilerParams(vmem_limit_bytes=VMEM_LIMIT),
    )(q, own, sib, residual, router_t, ids, ids.T)


def expert_kernel(
    experts, cap, n_seq,
    send_ref, state_ref, gate_ref, wgu_ref, wdn_ref, out_ref,
    recv, res, ret, wgu, wdn, acc,
    wsend, wrecv, wloc, lsem, dsend, drecv, bsend, brecv,
):
    branch = lax.axis_index("branch")
    seq = lax.axis_index("seq")
    core = seq % 2
    me = (branch * n_seq + seq) // 2
    pair = 2 * cap
    width = send_ref.shape[1]
    twin = {"seq": seq + 1 - 2 * core}
    mesh_id = pl.DeviceIdType.MESH

    def place(k):
        other = flipped(me, k, experts)
        return {"branch": (2 * other) // n_seq, "seq": (2 * other) % n_seq + core}

    barrier = pltpu.get_barrier_semaphore()
    pl.semaphore_signal(barrier, inc=1, device_id=twin, device_id_type=mesh_id)

    @pl.loop(1, experts)
    def _(k):
        pl.semaphore_signal(barrier, inc=1, device_id=place(k), device_id_type=mesh_id)

    pl.semaphore_wait(barrier, experts)

    def block(k):
        return pl.ds(pl.multiple_of(k * cap, 16), cap)

    def dispatch(k):
        return pltpu.make_async_remote_copy(
            src_ref=send_ref.at[block(k)], dst_ref=recv.at[block(k)],
            send_sem=dsend.at[k], recv_sem=drecv.at[k],
            device_id=place(k), device_id_type=mesh_id,
        )

    def give_back(k):
        return pltpu.make_async_remote_copy(
            src_ref=res.at[block(k)], dst_ref=ret.at[block(k)],
            send_sem=bsend.at[k], recv_sem=brecv.at[k],
            device_id=place(k), device_id_type=mesh_id,
        )

    weights = []
    for i, (src, dst) in enumerate(((wgu_ref, wgu), (wdn_ref, wdn))):
        weights.append(
            pltpu.make_async_remote_copy(
                src_ref=src, dst_ref=dst.at[1], send_sem=wsend.at[i], recv_sem=wrecv.at[i],
                device_id=twin, device_id_type=mesh_id,
            )
        )
        weights.append(pltpu.make_async_copy(src, dst.at[0], wloc.at[i]))
    dispatch(1).start()
    mine = pltpu.make_async_copy(send_ref.at[block(0)], recv.at[block(0)], lsem)
    mine.start()

    @pl.loop(experts // 2, experts)
    def _(k):
        dispatch(k).start()

    @pl.loop(2, experts // 2)
    def _(k):
        dispatch(k).start()

    for copy in weights:
        copy.start()
    acc[...] = state_ref[...]
    for copy in weights:
        copy.wait()

    chunk = 512

    def compute(p):
        span = pl.ds(pl.multiple_of(p * pair, 16), pair)
        acts = []
        for h in range(2):
            x = recv[span, :]
            gate = jnp.dot(x, wgu[h, 0], preferred_element_type=F32)
            up = jnp.dot(x, wgu[h, 1], preferred_element_type=F32)
            acts.append((gate / (1.0 + jnp.exp(-gate)) * up).astype(BF16))
        for start in range(0, width, chunk):
            cols = slice(start, start + chunk)
            done = jnp.dot(acts[0], wdn[0, :, cols], preferred_element_type=F32)
            done += jnp.dot(acts[1], wdn[1, :, cols], preferred_element_type=F32)
            res[span, cols] = done.astype(BF16)

    quarter = experts // 4

    def turn(i):
        return jnp.where(i <= quarter, i + quarter - 1, i - quarter)

    mine.wait()
    dispatch(1).wait_recv()
    compute(0)
    give_back(1).start()

    @pl.loop(1, experts // 2)
    def _(i):
        p = turn(i)
        dispatch(2 * p).wait_recv()
        dispatch(2 * p + 1).wait_recv()
        compute(p)
        give_back(2 * p).start()
        give_back(2 * p + 1).start()

    def add(p, rows):
        for start in range(0, width, chunk):
            cols = slice(start, start + chunk)
            block_rows = rows(cols)
            acc[:, cols] += jnp.dot(
                gate_ref[p, 0], block_rows, preferred_element_type=F32
            ) + jnp.dot(gate_ref[p, 1], block_rows, preferred_element_type=F32)

    give_back(1).wait_recv()
    add(0, lambda cols: jnp.concatenate([res[0:cap, cols], ret[cap:pair, cols]], axis=0))

    @pl.loop(1, experts // 2)
    def _(i):
        p = turn(i)
        give_back(2 * p).wait_recv()
        give_back(2 * p + 1).wait_recv()
        span = pl.ds(pl.multiple_of(p * pair, 16), pair)
        add(p, lambda cols: ret[span, cols])

    out_ref[...] = acc[...].astype(BF16)

    @pl.loop(1, experts)
    def _(k):
        dispatch(k).wait_send()
        give_back(k).wait_send()


def run_experts(send, state, gate, wgu, wdn, experts, cap, n_seq):
    rows, width = state.shape
    ff = wdn.shape[0]
    return pl.pallas_call(
        functools.partial(expert_kernel, experts, cap, n_seq),
        out_shape=jax.ShapeDtypeStruct((rows, width), BF16),
        in_specs=[ANY, VMEM, VMEM, ANY, ANY],
        out_specs=VMEM,
        scratch_shapes=[
            pltpu.VMEM((experts * cap, width), BF16),
            pltpu.VMEM((experts * cap, width), BF16),
            pltpu.VMEM((experts * cap, width), BF16),
            pltpu.VMEM((2, 2, width, ff), BF16),
            pltpu.VMEM((2, ff, width), BF16),
            pltpu.VMEM((rows, width), F32),
            pltpu.SemaphoreType.DMA((2,)),
            pltpu.SemaphoreType.DMA((2,)),
            pltpu.SemaphoreType.DMA((2,)),
            pltpu.SemaphoreType.DMA,
            pltpu.SemaphoreType.DMA((experts,)),
            pltpu.SemaphoreType.DMA((experts,)),
            pltpu.SemaphoreType.DMA((experts,)),
            pltpu.SemaphoreType.DMA((experts,)),
        ],
        compiler_params=pltpu.CompilerParams(
            collective_id=1, has_side_effects=True, vmem_limit_bytes=VMEM_LIMIT
        ),
    )(send, state, gate, wgu, wdn)


def on_device(
    n_branch, n_seq, queries, keyvals, residual, read_list, router, expert_ids, w_gate_up, w_down
):
    rows = queries.shape[1]
    experts = router.shape[1]
    top_count = expert_ids.shape[2]
    capacity = 2 * ((3 * rows * top_count + 4 * experts - 1) // (4 * experts))
    cap = (capacity + 15) // 16 * 16
    kv = keyvals.reshape(rows, -1)
    own, sib = exchange_kv(kv, read_list.reshape(-1), n_branch, n_seq)
    own = own.reshape(-1, kv.shape[1])
    sib = sib.reshape(-1, kv.shape[1])
    wgu = jnp.swapaxes(w_gate_up[0], 0, 1)
    send, state, gate = attend(
        queries[0], own, sib, residual[0], router.T, expert_ids[0], experts, cap, n_seq
    )
    return run_experts(send, state, gate, wgu, w_down[0], experts, cap, n_seq)[None]


def solution(mesh):
    return jax.shard_map(
        functools.partial(on_device, mesh.shape["branch"], mesh.shape["seq"]),
        mesh=mesh,
        in_specs=(
            P(("rollout", "branch"), "seq", None),
            P(("rollout", "branch"), "seq", None, None),
            P(("rollout", "branch"), "seq", None),
            P(("rollout", "branch"), "seq", None),
            P(),
            P(("rollout", "branch"), "seq", None),
            P(("branch", "seq"), None, None, None),
            P(("branch", "seq"), None, None),
        ),
        out_specs=P(("rollout", "branch"), "seq", None),
        check_vma=False,
    )
```

```python
import functools
import math

import jax
import jax.numpy as jnp
from jax import lax
from jax.experimental import pallas as pl
from jax.experimental.pallas import tpu as pltpu
from jax.sharding import PartitionSpec as P

HEAD_SIZE = 128
VMEM_LIMIT = 60 * 1024 * 1024
F32 = jnp.float32
BF16 = jnp.bfloat16
ANY = pl.BlockSpec(memory_space=pl.ANY)
VMEM = pl.BlockSpec(memory_space=pltpu.VMEM)
SMEM = pl.BlockSpec(memory_space=pltpu.SMEM)


def flipped(number, mask, count):
    value, bit = 0, 1
    while bit < count:
        value = value + ((number // bit + mask // bit) % 2) * bit
        bit *= 2
    return value


def attend_kernel(
    experts, cap, n_branch, n_seq,
    list_ref, q_ref, own_ref, res_ref, router_ref, ids_ref, idt_ref,
    send_ref, state_ref, gate_ref,
    picked, sib_ref, tops, totals, ssem, rsem,
):
    branch = lax.axis_index("branch")
    seq = lax.axis_index("seq")
    me = (branch * n_seq + seq) // 2
    rows, width = q_ref.shape
    kv_heads = own_ref.shape[2] // (2 * HEAD_SIZE)
    group = width // HEAD_SIZE // kv_heads
    together = 2
    tall = together * rows
    own_len = n_seq * rows
    sib_len = (n_branch - 1) * rows
    scale = 1.0 / math.sqrt(HEAD_SIZE)
    nt = (((1,), (1,)), ((), ()))

    barrier = pltpu.get_barrier_semaphore()
    for step in range(1, n_branch):
        pl.semaphore_signal(
            barrier, inc=1, device_id={"branch": (branch + step) % n_branch},
            device_id_type=pl.DeviceIdType.MESH,
        )
    for offset in range(n_branch - 1):
        picked[offset] = own_ref[(seq - list_ref[offset] + n_seq) % n_seq]
    pl.semaphore_wait(barrier, n_branch - 1)
    copies = []
    for offset in range(n_branch - 1):
        copy = pltpu.make_async_remote_copy(
            src_ref=picked.at[offset], dst_ref=sib_ref.at[offset],
            send_sem=ssem.at[offset], recv_sem=rsem.at[offset],
            device_id={"branch": (branch + offset + 1) % n_branch},
            device_id_type=pl.DeviceIdType.MESH,
        )
        copy.start()
        copies.append(copy)

    at_row = lax.broadcasted_iota(jnp.int32, (tall, own_len), 0) % rows
    at_col = lax.broadcasted_iota(jnp.int32, (tall, own_len), 1)
    earlier = at_col // rows
    bias = jnp.where(
        earlier == 0,
        jnp.where(at_col <= at_row, 0.0, -1e30),
        jnp.where(earlier <= seq, 0.0, -1e30),
    )

    def head_parts(head, step):
        base = (head * group + step * together) * HEAD_SIZE
        cols = [
            pl.ds(pl.multiple_of(base + i * HEAD_SIZE, HEAD_SIZE), HEAD_SIZE)
            for i in range(together)
        ]
        return cols, jnp.concatenate([q_ref[:, c] for c in cols], axis=0)

    def kv_cols(head):
        return (
            slice(head * HEAD_SIZE, (head + 1) * HEAD_SIZE),
            slice((kv_heads + head) * HEAD_SIZE, (kv_heads + head + 1) * HEAD_SIZE),
        )

    steps = group // together
    for head in range(kv_heads):
        kcol, vcol = kv_cols(head)

        @pl.loop(0, steps)
        def _(step):
            cols, q = head_parts(head, step)
            keys = own_ref[:, :, kcol].reshape(own_len, HEAD_SIZE)
            values = own_ref[:, :, vcol].reshape(own_len, HEAD_SIZE)
            scores = lax.dot_general(q, keys, nt, preferred_element_type=F32) * scale + bias
            top = jnp.max(scores, axis=1, keepdims=True)
            p = jnp.exp(scores - top)
            tops[head * steps + step] = top
            totals[head * steps + step] = jnp.sum(p, axis=1, keepdims=True)
            mixed = jnp.dot(p.astype(BF16), values, preferred_element_type=F32)
            for i, c in enumerate(cols):
                state_ref[:, c] = mixed[i * rows : (i + 1) * rows]

    for copy in copies:
        copy.wait()
    for head in range(kv_heads):
        kcol, vcol = kv_cols(head)

        @pl.loop(0, steps)
        def _(step):
            cols, q = head_parts(head, step)
            keys = sib_ref[:, :, kcol].reshape(sib_len, HEAD_SIZE)
            values = sib_ref[:, :, vcol].reshape(sib_len, HEAD_SIZE)
            scores = lax.dot_general(q, keys, nt, preferred_element_type=F32) * scale
            own_top = tops[head * steps + step]
            top = jnp.maximum(own_top, jnp.max(scores, axis=1, keepdims=True))
            p = jnp.exp(scores - top)
            shrink = jnp.exp(own_top - top)
            total = totals[head * steps + step] * shrink + jnp.sum(p, axis=1, keepdims=True)
            mixed = jnp.dot(p.astype(BF16), values, preferred_element_type=F32)
            inverse = 1.0 / total
            for i, c in enumerate(cols):
                part = slice(i * rows, (i + 1) * rows)
                context = (state_ref[:, c] * shrink[part] + mixed[part]) * inverse[part]
                state_ref[:, c] = res_ref[:, c].astype(F32) + context.astype(BF16).astype(F32)

    state = state_ref[...]
    normed = (
        state * lax.rsqrt(jnp.mean(state * state, axis=1, keepdims=True) + 1e-06)
    ).astype(BF16)
    logits = lax.dot_general(normed, router_ref[...], nt, preferred_element_type=F32)

    top_count = ids_ref.shape[1]
    ids, idt = ids_ref[...], idt_ref[...]
    kinds = lax.broadcasted_iota(jnp.int32, (rows, experts), 1)
    kinds_t = lax.broadcasted_iota(jnp.int32, (experts, rows), 0)
    hot = [(ids[:, k : k + 1] == kinds).astype(F32) for k in range(top_count)]
    hot_t = [(idt[k : k + 1, :] == kinds_t).astype(F32) for k in range(top_count)]
    down = lax.broadcasted_iota(jnp.int32, (rows, rows), 0)
    along = lax.broadcasted_iota(jnp.int32, (rows, rows), 1)
    before = jnp.dot((along < down).astype(F32).astype(BF16), sum(hot).astype(BF16), preferred_element_type=F32)
    before_t = jnp.dot(sum(hot_t).astype(BF16), (down < along).astype(F32).astype(BF16), preferred_element_type=F32)
    dest, dest_t = [], []
    for k in range(top_count):
        slot = jnp.sum(before * hot[k], axis=1, keepdims=True).astype(jnp.int32)
        dest.append((ids[:, k : k + 1] ^ me) * cap + slot)
        slot_t = jnp.sum(before_t * hot_t[k], axis=0, keepdims=True).astype(jnp.int32)
        dest_t.append((idt[k : k + 1, :] ^ me) * cap + slot_t)
    chosen = [jnp.sum(logits * hot[k], axis=1, keepdims=True) for k in range(top_count)]
    gates = [1.0 / sum(jnp.exp(c - chosen[k]) for c in chosen) for k in range(top_count)]

    pair = 2 * cap
    places = lax.broadcasted_iota(jnp.int32, (rows, pair), 1)
    places_t = lax.broadcasted_iota(jnp.int32, (pair, rows), 0)
    for p in range(experts // 2):
        pick = sum((dest_t[k] - p * pair == places_t).astype(F32) for k in range(top_count))
        send_ref[p * pair : (p + 1) * pair, :] = jnp.dot(
            pick.astype(BF16), normed, preferred_element_type=F32
        ).astype(BF16)
        weight = sum(
            jnp.where(dest[k] - p * pair == places, gates[k], 0.0) for k in range(top_count)
        )
        high = weight.astype(BF16)
        gate_ref[p, 0] = high
        gate_ref[p, 1] = (weight - high.astype(F32)).astype(BF16)


def attend(listed, q, own, residual, router_t, ids, experts, cap, n_branch, n_seq):
    rows, width = q.shape
    halves = width // HEAD_SIZE // 2
    return pl.pallas_call(
        functools.partial(attend_kernel, experts, cap, n_branch, n_seq),
        out_shape=(
            jax.ShapeDtypeStruct((experts * cap, width), BF16),
            jax.ShapeDtypeStruct((rows, width), F32),
            jax.ShapeDtypeStruct((experts // 2, 2, rows, 2 * cap), BF16),
        ),
        in_specs=[SMEM] + [VMEM] * 6,
        out_specs=(VMEM, VMEM, VMEM),
        scratch_shapes=[
            pltpu.VMEM((n_branch - 1, rows, own.shape[2]), BF16),
            pltpu.VMEM((n_branch - 1, rows, own.shape[2]), BF16),
            pltpu.VMEM((halves, 2 * rows, 1), F32),
            pltpu.VMEM((halves, 2 * rows, 1), F32),
            pltpu.SemaphoreType.DMA((n_branch,)),
            pltpu.SemaphoreType.DMA((n_branch,)),
        ],
        compiler_params=pltpu.CompilerParams(
            collective_id=0, has_side_effects=True, vmem_limit_bytes=VMEM_LIMIT
        ),
    )(listed, q, own, residual, router_t, ids, ids.T)


def expert_kernel(
    experts, cap, n_seq,
    send_ref, state_ref, gate_ref, wgu_ref, wdn_ref, out_ref,
    recv, res, ret, wgu, wdn, acc,
    wsend, wrecv, wloc, lsem, dsend, drecv, bsend, brecv,
):
    branch = lax.axis_index("branch")
    seq = lax.axis_index("seq")
    core = seq % 2
    me = (branch * n_seq + seq) // 2
    pair = 2 * cap
    width = send_ref.shape[1]
    twin = {"seq": seq + 1 - 2 * core}
    mesh_id = pl.DeviceIdType.MESH

    def place(k):
        other = flipped(me, k, experts)
        return {"branch": (2 * other) // n_seq, "seq": (2 * other) % n_seq + core}

    barrier = pltpu.get_barrier_semaphore()
    pl.semaphore_signal(barrier, inc=1, device_id=twin, device_id_type=mesh_id)

    @pl.loop(1, experts)
    def _(k):
        pl.semaphore_signal(barrier, inc=1, device_id=place(k), device_id_type=mesh_id)

    pl.semaphore_wait(barrier, experts)

    def block(k):
        return pl.ds(pl.multiple_of(k * cap, 16), cap)

    def dispatch(k):
        return pltpu.make_async_remote_copy(
            src_ref=send_ref.at[block(k)], dst_ref=recv.at[block(k)],
            send_sem=dsend.at[k], recv_sem=drecv.at[k],
            device_id=place(k), device_id_type=mesh_id,
        )

    def give_back(k):
        return pltpu.make_async_remote_copy(
            src_ref=res.at[block(k)], dst_ref=ret.at[block(k)],
            send_sem=bsend.at[k], recv_sem=brecv.at[k],
            device_id=place(k), device_id_type=mesh_id,
        )

    weights = []
    for i, (src, dst) in enumerate(((wgu_ref, wgu), (wdn_ref, wdn))):
        weights.append(
            pltpu.make_async_remote_copy(
                src_ref=src, dst_ref=dst.at[1], send_sem=wsend.at[i], recv_sem=wrecv.at[i],
                device_id=twin, device_id_type=mesh_id,
            )
        )
        weights.append(pltpu.make_async_copy(src, dst.at[0], wloc.at[i]))
    dispatch(1).start()
    mine = pltpu.make_async_copy(send_ref.at[block(0)], recv.at[block(0)], lsem)
    mine.start()

    @pl.loop(experts // 2, experts)
    def _(k):
        dispatch(k).start()

    @pl.loop(2, experts // 2)
    def _(k):
        dispatch(k).start()

    for copy in weights:
        copy.start()
    acc[...] = state_ref[...]
    for copy in weights:
        copy.wait()

    chunk = 512

    def compute(p):
        span = pl.ds(pl.multiple_of(p * pair, 16), pair)
        acts = []
        for h in range(2):
            x = recv[span, :]
            gate = jnp.dot(x, wgu[h, 0], preferred_element_type=F32)
            up = jnp.dot(x, wgu[h, 1], preferred_element_type=F32)
            acts.append((gate / (1.0 + jnp.exp(-gate)) * up).astype(BF16))
        for start in range(0, width, chunk):
            cols = slice(start, start + chunk)
            done = jnp.dot(acts[0], wdn[0, :, cols], preferred_element_type=F32)
            done += jnp.dot(acts[1], wdn[1, :, cols], preferred_element_type=F32)
            res[span, cols] = done.astype(BF16)

    quarter = experts // 4

    def turn(i):
        return jnp.where(i <= quarter, i + quarter - 1, i - quarter)

    mine.wait()
    dispatch(1).wait_recv()
    compute(0)
    give_back(1).start()

    @pl.loop(1, experts // 2)
    def _(i):
        p = turn(i)
        dispatch(2 * p).wait_recv()
        dispatch(2 * p + 1).wait_recv()
        compute(p)
        give_back(2 * p).start()
        give_back(2 * p + 1).start()

    def add(p, rows):
        for start in range(0, width, chunk):
            cols = slice(start, start + chunk)
            block_rows = rows(cols)
            acc[:, cols] += jnp.dot(
                gate_ref[p, 0], block_rows, preferred_element_type=F32
            ) + jnp.dot(gate_ref[p, 1], block_rows, preferred_element_type=F32)

    give_back(1).wait_recv()
    add(0, lambda cols: jnp.concatenate([res[0:cap, cols], ret[cap:pair, cols]], axis=0))

    @pl.loop(1, experts // 2)
    def _(i):
        p = turn(i)
        give_back(2 * p).wait_recv()
        give_back(2 * p + 1).wait_recv()
        span = pl.ds(pl.multiple_of(p * pair, 16), pair)
        add(p, lambda cols: ret[span, cols])

    out_ref[...] = acc[...].astype(BF16)

    @pl.loop(1, experts)
    def _(k):
        dispatch(k).wait_send()
        give_back(k).wait_send()


def run_experts(send, state, gate, wgu, wdn, experts, cap, n_seq):
    rows, width = state.shape
    ff = wdn.shape[0]
    return pl.pallas_call(
        functools.partial(expert_kernel, experts, cap, n_seq),
        out_shape=jax.ShapeDtypeStruct((rows, width), BF16),
        in_specs=[ANY, VMEM, VMEM, ANY, ANY],
        out_specs=VMEM,
        scratch_shapes=[
            pltpu.VMEM((experts * cap, width), BF16),
            pltpu.VMEM((experts * cap, width), BF16),
            pltpu.VMEM((experts * cap, width), BF16),
            pltpu.VMEM((2, 2, width, ff), BF16),
            pltpu.VMEM((2, ff, width), BF16),
            pltpu.VMEM((rows, width), F32),
            pltpu.SemaphoreType.DMA((2,)),
            pltpu.SemaphoreType.DMA((2,)),
            pltpu.SemaphoreType.DMA((2,)),
            pltpu.SemaphoreType.DMA,
            pltpu.SemaphoreType.DMA((experts,)),
            pltpu.SemaphoreType.DMA((experts,)),
            pltpu.SemaphoreType.DMA((experts,)),
            pltpu.SemaphoreType.DMA((experts,)),
        ],
        compiler_params=pltpu.CompilerParams(
            collective_id=1, has_side_effects=True, vmem_limit_bytes=VMEM_LIMIT
        ),
    )(send, state, gate, wgu, wdn)


def on_device(
    n_branch, n_seq, queries, keyvals, residual, read_list, router, expert_ids, w_gate_up, w_down
):
    rows = queries.shape[1]
    experts = router.shape[1]
    top_count = expert_ids.shape[2]
    capacity = 2 * ((3 * rows * top_count + 4 * experts - 1) // (4 * experts))
    cap = (capacity + 15) // 16 * 16
    kv = keyvals.reshape(rows, -1)
    shifts = [
        lax.ppermute(kv, "seq", [(i, (i + step) % n_seq) for i in range(n_seq)])
        for step in range(1, n_seq)
    ]
    own = jnp.stack([kv] + shifts)
    wgu = jnp.swapaxes(w_gate_up[0], 0, 1)
    send, state, gate = attend(
        read_list.reshape(-1), queries[0], own, residual[0], router.T, expert_ids[0],
        experts, cap, n_branch, n_seq,
    )
    return run_experts(send, state, gate, wgu, w_down[0], experts, cap, n_seq)[None]


def solution(mesh):
    return jax.shard_map(
        functools.partial(on_device, mesh.shape["branch"], mesh.shape["seq"]),
        mesh=mesh,
        in_specs=(
            P(("rollout", "branch"), "seq", None),
            P(("rollout", "branch"), "seq", None, None),
            P(("rollout", "branch"), "seq", None),
            P(("rollout", "branch"), "seq", None),
            P(),
            P(("rollout", "branch"), "seq", None),
            P(("branch", "seq"), None, None, None),
            P(("branch", "seq"), None, None),
        ),
        out_specs=P(("rollout", "branch"), "seq", None),
        check_vma=False,
    )
```

```python
import functools
import math

import jax
import jax.numpy as jnp
from jax import lax
from jax.experimental import pallas as pl
from jax.experimental.pallas import tpu as pltpu
from jax.sharding import PartitionSpec as P

HEAD_SIZE = 128
PARTS = 4
VMEM_LIMIT = 60 * 1024 * 1024
F32 = jnp.float32
BF16 = jnp.bfloat16
ANY = pl.BlockSpec(memory_space=pl.ANY)
VMEM = pl.BlockSpec(memory_space=pltpu.VMEM)
SMEM = pl.BlockSpec(memory_space=pltpu.SMEM)


def flipped(number, mask, count):
    value, bit = 0, 1
    while bit < count:
        value = value + ((number // bit + mask // bit) % 2) * bit
        bit *= 2
    return value


def attend_kernel(
    experts, cap, n_branch, n_seq,
    list_ref, q_ref, own_ref, res_ref, router_ref, ids_ref, idt_ref,
    send_ref, state_ref, gate_ref, norm_ref, meta_ref,
    picked, sib_ref, tops, totals, ssem, rsem,
):
    branch = lax.axis_index("branch")
    seq = lax.axis_index("seq")
    me = (branch * n_seq + seq) // 2
    rows, width = q_ref.shape
    kv_heads = own_ref.shape[2] // (2 * HEAD_SIZE)
    group = width // HEAD_SIZE // kv_heads
    together = 2
    tall = together * rows
    own_len = n_seq * rows
    sib_len = (n_branch - 1) * rows
    scale = 1.0 / math.sqrt(HEAD_SIZE)
    nt = (((1,), (1,)), ((), ()))

    barrier = pltpu.get_barrier_semaphore()
    for step in range(1, n_branch):
        pl.semaphore_signal(
            barrier, inc=1, device_id={"branch": (branch + step) % n_branch},
            device_id_type=pl.DeviceIdType.MESH,
        )
    for offset in range(n_branch - 1):
        picked[offset] = own_ref[(seq - list_ref[offset] + n_seq) % n_seq]
    pl.semaphore_wait(barrier, n_branch - 1)
    copies = []
    for offset in range(n_branch - 1):
        copy = pltpu.make_async_remote_copy(
            src_ref=picked.at[offset], dst_ref=sib_ref.at[offset],
            send_sem=ssem.at[offset], recv_sem=rsem.at[offset],
            device_id={"branch": (branch + offset + 1) % n_branch},
            device_id_type=pl.DeviceIdType.MESH,
        )
        copy.start()
        copies.append(copy)

    at_row = lax.broadcasted_iota(jnp.int32, (tall, own_len), 0) % rows
    at_col = lax.broadcasted_iota(jnp.int32, (tall, own_len), 1)
    earlier = at_col // rows
    bias = jnp.where(
        earlier == 0,
        jnp.where(at_col <= at_row, 0.0, -1e30),
        jnp.where(earlier <= seq, 0.0, -1e30),
    )

    def head_parts(head, step):
        base = (head * group + step * together) * HEAD_SIZE
        cols = [
            pl.ds(pl.multiple_of(base + i * HEAD_SIZE, HEAD_SIZE), HEAD_SIZE)
            for i in range(together)
        ]
        return cols, jnp.concatenate([q_ref[:, c] for c in cols], axis=0)

    def kv_cols(head):
        return (
            slice(head * HEAD_SIZE, (head + 1) * HEAD_SIZE),
            slice((kv_heads + head) * HEAD_SIZE, (kv_heads + head + 1) * HEAD_SIZE),
        )

    steps = group // together
    for head in range(kv_heads):
        kcol, vcol = kv_cols(head)

        @pl.loop(0, steps)
        def _(step):
            cols, q = head_parts(head, step)
            keys = own_ref[:, :, kcol].reshape(own_len, HEAD_SIZE)
            values = own_ref[:, :, vcol].reshape(own_len, HEAD_SIZE)
            scores = lax.dot_general(q, keys, nt, preferred_element_type=F32) * scale + bias
            top = jnp.max(scores, axis=1, keepdims=True)
            p = jnp.exp(scores - top)
            tops[head * steps + step] = top
            totals[head * steps + step] = jnp.sum(p, axis=1, keepdims=True)
            mixed = jnp.dot(p.astype(BF16), values, preferred_element_type=F32)
            for i, c in enumerate(cols):
                state_ref[:, c] = mixed[i * rows : (i + 1) * rows]

    for copy in copies:
        copy.wait()
    for head in range(kv_heads):
        kcol, vcol = kv_cols(head)

        @pl.loop(0, steps)
        def _(step):
            cols, q = head_parts(head, step)
            keys = sib_ref[:, :, kcol].reshape(sib_len, HEAD_SIZE)
            values = sib_ref[:, :, vcol].reshape(sib_len, HEAD_SIZE)
            scores = lax.dot_general(q, keys, nt, preferred_element_type=F32) * scale
            own_top = tops[head * steps + step]
            top = jnp.maximum(own_top, jnp.max(scores, axis=1, keepdims=True))
            p = jnp.exp(scores - top)
            shrink = jnp.exp(own_top - top)
            total = totals[head * steps + step] * shrink + jnp.sum(p, axis=1, keepdims=True)
            mixed = jnp.dot(p.astype(BF16), values, preferred_element_type=F32)
            inverse = 1.0 / total
            for i, c in enumerate(cols):
                part = slice(i * rows, (i + 1) * rows)
                context = (state_ref[:, c] * shrink[part] + mixed[part]) * inverse[part]
                state_ref[:, c] = res_ref[:, c].astype(F32) + context.astype(BF16).astype(F32)

    state = state_ref[...]
    normed = (
        state * lax.rsqrt(jnp.mean(state * state, axis=1, keepdims=True) + 1e-06)
    ).astype(BF16)
    logits = lax.dot_general(normed, router_ref[...], nt, preferred_element_type=F32)

    top_count = ids_ref.shape[1]
    ids, idt = ids_ref[...], idt_ref[...]
    kinds = lax.broadcasted_iota(jnp.int32, (rows, experts), 1)
    kinds_t = lax.broadcasted_iota(jnp.int32, (experts, rows), 0)
    hot = [(ids[:, k : k + 1] == kinds).astype(F32) for k in range(top_count)]
    hot_t = [(idt[k : k + 1, :] == kinds_t).astype(F32) for k in range(top_count)]
    down = lax.broadcasted_iota(jnp.int32, (rows, rows), 0)
    along = lax.broadcasted_iota(jnp.int32, (rows, rows), 1)
    before = jnp.dot((along < down).astype(F32).astype(BF16), sum(hot).astype(BF16), preferred_element_type=F32)
    before_t = jnp.dot(sum(hot_t).astype(BF16), (down < along).astype(F32).astype(BF16), preferred_element_type=F32)
    dest, dest_t = [], []
    for k in range(top_count):
        slot = jnp.sum(before * hot[k], axis=1, keepdims=True).astype(jnp.int32)
        dest.append((ids[:, k : k + 1] ^ me) * cap + slot)
        slot_t = jnp.sum(before_t * hot_t[k], axis=0, keepdims=True).astype(jnp.int32)
        dest_t.append((idt[k : k + 1, :] ^ me) * cap + slot_t)
    chosen = [jnp.sum(logits * hot[k], axis=1, keepdims=True) for k in range(top_count)]
    gates = [1.0 / sum(jnp.exp(c - chosen[k]) for c in chosen) for k in range(top_count)]

    parts, _, part_width = norm_ref.shape
    for c in range(parts):
        norm_ref[c] = normed[:, c * part_width : (c + 1) * part_width]
    logits_t = lax.dot_general(router_ref[...], normed, nt, preferred_element_type=F32)
    chosen_t = [jnp.sum(logits_t * hot_t[k], axis=0, keepdims=True) for k in range(top_count)]
    meta_ref[...] = jnp.zeros_like(meta_ref)
    for k in range(top_count):
        meta_ref[k : k + 1, :] = dest_t[k].astype(F32)
        meta_ref[top_count + k : top_count + k + 1, :] = 1.0 / sum(
            jnp.exp(c - chosen_t[k]) for c in chosen_t
        )

    pair = 2 * cap
    places = lax.broadcasted_iota(jnp.int32, (rows, pair), 1)
    places_t = lax.broadcasted_iota(jnp.int32, (pair, rows), 0)
    for p in range(send_ref.shape[0] // pair):
        pick = sum((dest_t[k] - p * pair == places_t).astype(F32) for k in range(top_count))
        send_ref[p * pair : (p + 1) * pair, :] = jnp.dot(
            pick.astype(BF16), normed, preferred_element_type=F32
        ).astype(BF16)
        weight = sum(
            jnp.where(dest[k] - p * pair == places, gates[k], 0.0) for k in range(top_count)
        )
        high = weight.astype(BF16)
        gate_ref[p, 0] = high
        gate_ref[p, 1] = (weight - high.astype(F32)).astype(BF16)


def attend(listed, q, own, residual, router_t, ids, experts, near, cap, n_branch, n_seq):
    rows, width = q.shape
    halves = width // HEAD_SIZE // 2
    return pl.pallas_call(
        functools.partial(attend_kernel, experts, cap, n_branch, n_seq),
        out_shape=(
            jax.ShapeDtypeStruct((near * cap, width), BF16),
            jax.ShapeDtypeStruct((rows, width), F32),
            jax.ShapeDtypeStruct((near // 2, 2, rows, 2 * cap), BF16),
            jax.ShapeDtypeStruct((PARTS, rows, width // PARTS), BF16),
            jax.ShapeDtypeStruct((8, rows), F32),
        ),
        in_specs=[SMEM] + [VMEM] * 6,
        out_specs=(VMEM,) * 5,
        scratch_shapes=[
            pltpu.VMEM((n_branch - 1, rows, own.shape[2]), BF16),
            pltpu.VMEM((n_branch - 1, rows, own.shape[2]), BF16),
            pltpu.VMEM((halves, 2 * rows, 1), F32),
            pltpu.VMEM((halves, 2 * rows, 1), F32),
            pltpu.SemaphoreType.DMA((n_branch,)),
            pltpu.SemaphoreType.DMA((n_branch,)),
        ],
        compiler_params=pltpu.CompilerParams(
            collective_id=0, has_side_effects=True, vmem_limit_bytes=VMEM_LIMIT
        ),
    )(listed, q, own, residual, router_t, ids, ids.T)


def expert_kernel(
    experts, cap, n_seq,
    send_ref, state_ref, gate_ref, wgu_ref, wdn_ref, out_ref,
    recv, res, ret, wgu, wdn, acc,
    wsend, wrecv, wloc, lsem, dsend, drecv, bsend, brecv,
):
    branch = lax.axis_index("branch")
    seq = lax.axis_index("seq")
    core = seq % 2
    me = (branch * n_seq + seq) // 2
    pair = 2 * cap
    width = send_ref.shape[1]
    twin = {"seq": seq + 1 - 2 * core}
    mesh_id = pl.DeviceIdType.MESH

    def place(k):
        other = flipped(me, k, experts)
        return {"branch": (2 * other) // n_seq, "seq": (2 * other) % n_seq + core}

    barrier = pltpu.get_barrier_semaphore()
    pl.semaphore_signal(barrier, inc=1, device_id=twin, device_id_type=mesh_id)

    @pl.loop(1, experts)
    def _(k):
        pl.semaphore_signal(barrier, inc=1, device_id=place(k), device_id_type=mesh_id)

    pl.semaphore_wait(barrier, experts)

    def block(k):
        return pl.ds(pl.multiple_of(k * cap, 16), cap)

    def dispatch(k):
        return pltpu.make_async_remote_copy(
            src_ref=send_ref.at[block(k)], dst_ref=recv.at[block(k)],
            send_sem=dsend.at[k], recv_sem=drecv.at[k],
            device_id=place(k), device_id_type=mesh_id,
        )

    def give_back(k):
        return pltpu.make_async_remote_copy(
            src_ref=res.at[block(k)], dst_ref=ret.at[block(k)],
            send_sem=bsend.at[k], recv_sem=brecv.at[k],
            device_id=place(k), device_id_type=mesh_id,
        )

    weights = []
    for i, (src, dst) in enumerate(((wgu_ref, wgu), (wdn_ref, wdn))):
        weights.append(
            pltpu.make_async_remote_copy(
                src_ref=src, dst_ref=dst.at[1], send_sem=wsend.at[i], recv_sem=wrecv.at[i],
                device_id=twin, device_id_type=mesh_id,
            )
        )
        weights.append(pltpu.make_async_copy(src, dst.at[0], wloc.at[i]))
    dispatch(1).start()
    mine = pltpu.make_async_copy(send_ref.at[block(0)], recv.at[block(0)], lsem)
    mine.start()

    @pl.loop(experts // 2, experts)
    def _(k):
        dispatch(k).start()

    @pl.loop(2, experts // 2)
    def _(k):
        dispatch(k).start()

    for copy in weights:
        copy.start()
    acc[...] = state_ref[...]
    for copy in weights:
        copy.wait()

    chunk = 512

    def compute(p):
        span = pl.ds(pl.multiple_of(p * pair, 16), pair)
        acts = []
        for h in range(2):
            x = recv[span, :]
            gate = jnp.dot(x, wgu[h, 0], preferred_element_type=F32)
            up = jnp.dot(x, wgu[h, 1], preferred_element_type=F32)
            acts.append((gate / (1.0 + jnp.exp(-gate)) * up).astype(BF16))
        for start in range(0, width, chunk):
            cols = slice(start, start + chunk)
            done = jnp.dot(acts[0], wdn[0, :, cols], preferred_element_type=F32)
            done += jnp.dot(acts[1], wdn[1, :, cols], preferred_element_type=F32)
            res[span, cols] = done.astype(BF16)

    quarter = experts // 4

    def turn(i):
        return jnp.where(i <= quarter, i + quarter - 1, i - quarter)

    mine.wait()
    dispatch(1).wait_recv()
    compute(0)
    give_back(1).start()

    @pl.loop(1, experts // 2)
    def _(i):
        p = turn(i)
        dispatch(2 * p).wait_recv()
        dispatch(2 * p + 1).wait_recv()
        compute(p)
        give_back(2 * p).start()
        give_back(2 * p + 1).start()

    def add(p, rows):
        for start in range(0, width, chunk):
            cols = slice(start, start + chunk)
            block_rows = rows(cols)
            acc[:, cols] += jnp.dot(
                gate_ref[p, 0], block_rows, preferred_element_type=F32
            ) + jnp.dot(gate_ref[p, 1], block_rows, preferred_element_type=F32)

    give_back(1).wait_recv()
    add(0, lambda cols: jnp.concatenate([res[0:cap, cols], ret[cap:pair, cols]], axis=0))

    @pl.loop(1, experts // 2)
    def _(i):
        p = turn(i)
        give_back(2 * p).wait_recv()
        give_back(2 * p + 1).wait_recv()
        span = pl.ds(pl.multiple_of(p * pair, 16), pair)
        add(p, lambda cols: ret[span, cols])

    out_ref[...] = acc[...].astype(BF16)

    @pl.loop(1, experts)
    def _(k):
        dispatch(k).wait_send()
        give_back(k).wait_send()


def run_experts(send, state, gate, wgu, wdn, experts, cap, n_seq):
    rows, width = state.shape
    ff = wdn.shape[0]
    return pl.pallas_call(
        functools.partial(expert_kernel, experts, cap, n_seq),
        out_shape=jax.ShapeDtypeStruct((rows, width), BF16),
        in_specs=[ANY, VMEM, VMEM, ANY, ANY],
        out_specs=VMEM,
        scratch_shapes=[
            pltpu.VMEM((experts * cap, width), BF16),
            pltpu.VMEM((experts * cap, width), BF16),
            pltpu.VMEM((experts * cap, width), BF16),
            pltpu.VMEM((2, 2, width, ff), BF16),
            pltpu.VMEM((2, ff, width), BF16),
            pltpu.VMEM((rows, width), F32),
            pltpu.SemaphoreType.DMA((2,)),
            pltpu.SemaphoreType.DMA((2,)),
            pltpu.SemaphoreType.DMA((2,)),
            pltpu.SemaphoreType.DMA,
            pltpu.SemaphoreType.DMA((experts,)),
            pltpu.SemaphoreType.DMA((experts,)),
            pltpu.SemaphoreType.DMA((experts,)),
            pltpu.SemaphoreType.DMA((experts,)),
        ],
        compiler_params=pltpu.CompilerParams(
            collective_id=1, has_side_effects=True, vmem_limit_bytes=VMEM_LIMIT
        ),
    )(send, state, gate, wgu, wdn)


def relay_kernel(
    cap, n_seq,
    send_ref, state_ref, gate_ref, norm_ref, meta_ref, wgu_ref, wdn_ref, out_ref,
    recv, res, ret, wgu, wdn, acc, xin, xmeta, fwd, rbuf, xout, far,
    wsend, wrecv, wloc, lsem, dsend, drecv, bsend, brecv,
    csend, crecv, msend, mrecv, fsend, rsend, rrecv, osend, orecv,
):
    experts, near = 8, 4
    branch = lax.axis_index("branch")
    seq = lax.axis_index("seq")
    core = seq % 2
    me = (branch * n_seq + seq) // 2
    inner = (branch + 1) // 2 % 2
    pair = 2 * cap
    rows, width = state_ref.shape
    step = width // PARTS
    twin = {"seq": seq + 1 - 2 * core}
    mesh_id = pl.DeviceIdType.MESH

    def place(k):
        other = flipped(me, k, experts)
        return {"branch": (2 * other) // n_seq, "seq": (2 * other) % n_seq + core}

    barrier = pltpu.get_barrier_semaphore()
    pl.semaphore_signal(barrier, inc=1, device_id=twin, device_id_type=mesh_id)
    for k in range(1, experts):
        pl.semaphore_signal(barrier, inc=1, device_id=place(k), device_id_type=mesh_id)
    pl.semaphore_wait(barrier, experts)

    def block(k):
        return pl.ds(pl.multiple_of(k * cap, 16), cap)

    def remote(src, dst, send, arrive, k):
        return pltpu.make_async_remote_copy(
            src_ref=src, dst_ref=dst, send_sem=send, recv_sem=arrive,
            device_id=place(k), device_id_type=mesh_id,
        )

    def dispatch(k):
        return remote(send_ref.at[block(k)], recv.at[block(k)], dsend.at[k], drecv.at[k], k)

    def give_back(k):
        return remote(res.at[block(k)], ret.at[block(k)], bsend.at[k], brecv.at[k], k)

    across = 4 + 2 * inner

    def cross(c):
        return remote(norm_ref.at[c], xin.at[1 - inner, c], csend.at[c], crecv.at[1 - inner, c], across)

    def cross_meta():
        return remote(meta_ref, xmeta.at[1 - inner], msend, mrecv.at[1 - inner], across)

    def arrived(s, c):
        return remote(norm_ref.at[c], xin.at[s, c], csend.at[c], crecv.at[s, c], across)

    def slot_of(s, f):
        return f ^ (6 - 2 * s)

    def part(c):
        return slice(c * step, (c + 1) * step)

    def forward(s, f, c):
        k = slot_of(s, f)
        src = fwd.at[s, f, :, part(c)]
        dst = recv.at[block(k), part(c)]
        if f == 0:
            return pltpu.make_async_copy(src, dst, drecv.at[k])
        return remote(src, dst, fsend.at[s, f], drecv.at[k], f)

    def got(k):
        remote(recv.at[block(k)], recv.at[block(k)], dsend.at[k], drecv.at[k], 1).wait_recv()

    weights = []
    for i, (src, dst) in enumerate(((wgu_ref, wgu), (wdn_ref, wdn))):
        weights.append(
            pltpu.make_async_remote_copy(
                src_ref=src, dst_ref=dst.at[1], send_sem=wsend.at[i], recv_sem=wrecv.at[i],
                device_id=twin, device_id_type=mesh_id,
            )
        )
        weights.append(pltpu.make_async_copy(src, dst.at[0], wloc.at[i]))

    def start_cross():
        cross_meta().start()
        for c in range(PARTS):
            cross(c).start()

    pl.when(inner == 1)(start_cross)
    mine = pltpu.make_async_copy(send_ref.at[block(0)], recv.at[block(0)], lsem)
    mine.start()
    for k in (1, 2, 3):
        dispatch(k).start()
    pl.when(inner == 0)(start_cross)
    for copy in weights:
        copy.start()
    acc[...] = state_ref[...]

    def rows_of(s):
        where = lax.broadcasted_iota(jnp.int32, (cap, rows), 0).astype(F32)
        meta = xmeta[s]
        return meta, [where + float(slot_of(s, f) * cap) for f in range(near)]

    def relay(s):
        remote(meta_ref, xmeta.at[s], msend, mrecv.at[s], across).wait_recv()
        meta, where = rows_of(s)
        pick = jnp.concatenate(
            [(meta[0:1] == w).astype(F32) + (meta[1:2] == w).astype(F32) for w in where], axis=0
        ).astype(BF16)
        for c in range(PARTS):
            arrived(s, c).wait_recv()
            taken = jnp.dot(pick, xin[s, c], preferred_element_type=F32).astype(BF16)
            for f in range(near):
                fwd[s, f, :, part(c)] = taken[f * cap : (f + 1) * cap]
            for f in (2, 3, 1, 0):
                forward(s, f, c).start()

    def hand(s, f, c, k):
        src = res.at[block(k), part(c)]
        dst = rbuf.at[s, f, :, part(c)]
        if f == 0:
            return pltpu.make_async_copy(src, dst, rrecv.at[s, f, c])
        return remote(src, dst, rsend.at[s, f, c], rrecv.at[s, f, c], f)

    def compute(p, after=None):
        span = pl.ds(pl.multiple_of(p * pair, 16), pair)
        acts = []
        for h in range(2):
            x = recv[span, :]
            gate = jnp.dot(x, wgu[h, 0], preferred_element_type=F32)
            up = jnp.dot(x, wgu[h, 1], preferred_element_type=F32)
            acts.append((gate / (1.0 + jnp.exp(-gate)) * up).astype(BF16))
        for c in range(PARTS):
            done = jnp.dot(acts[0], wdn[0, :, part(c)], preferred_element_type=F32)
            done += jnp.dot(acts[1], wdn[1, :, part(c)], preferred_element_type=F32)
            res[span, part(c)] = done.astype(BF16)
            if after is not None:
                after(c)

    pl.when(inner == 1)(lambda: relay(0))
    for copy in weights:
        copy.wait()
    mine.wait()
    got(1)
    compute(0)
    give_back(1).start()
    got(2)
    got(3)
    compute(1)
    give_back(2).start()
    give_back(3).start()
    pl.when(inner == 1)(lambda: relay(1))

    def far_group(s, base):
        def after(c):
            for f in (base, base + 1):
                hand(s, f, c, slot_of(s, f)).start()

        k = slot_of(s, base) // 2 * 2
        got(k)
        got(k + 1)
        compute(k // 2, after)

    for s in range(2):
        pl.when(inner == 1)(functools.partial(far_group, s, 0))
        pl.when(inner == 0)(functools.partial(far_group, s, 2))

    def result(s, c):
        return remote(xout.at[s, c], far.at[c], osend.at[s, c], orecv.at[c], 6 - 2 * s)

    def combine(s):
        meta, where = rows_of(s)
        weight = jnp.concatenate(
            [
                jnp.where(meta[0:1] == w, meta[2:3], 0.0) + jnp.where(meta[1:2] == w, meta[3:4], 0.0)
                for w in where
            ],
            axis=0,
        ).T
        high = weight.astype(BF16)
        low = (weight - high.astype(F32)).astype(BF16)
        for c in range(PARTS):
            for f in range(near):
                if f == 0:
                    hand(s, 0, c, slot_of(s, 0)).wait()
                else:
                    hand(s, f, c, slot_of(s, f)).wait_recv()
            given = rbuf[s, :, :, part(c)].reshape(near * cap, step)
            xout[s, c] = (
                jnp.dot(high, given, preferred_element_type=F32)
                + jnp.dot(low, given, preferred_element_type=F32)
            ).astype(BF16)
            result(s, c).start()

    def combine_all():
        combine(0)
        combine(1)

    pl.when(inner == 1)(combine_all)

    for p in range(near // 2):
        for k in (2 * p, 2 * p + 1):
            if k:
                give_back(k).wait_recv()
        for c in range(PARTS):
            cols = part(c)
            low = res if p == 0 else ret
            given = jnp.concatenate(
                [low[2 * p * cap : (2 * p + 1) * cap, cols], ret[(2 * p + 1) * cap : (2 * p + 2) * cap, cols]],
                axis=0,
            )
            acc[:, cols] += jnp.dot(gate_ref[p, 0], given, preferred_element_type=F32) + jnp.dot(
                gate_ref[p, 1], given, preferred_element_type=F32
            )
    for c in range(PARTS):
        result(0, c).wait_recv()
        out_ref[:, part(c)] = (acc[:, part(c)] + far[c].astype(F32)).astype(BF16)

    for k in (1, 2, 3):
        dispatch(k).wait_send()
        give_back(k).wait_send()
    cross_meta().wait_send()
    for c in range(PARTS):
        cross(c).wait_send()

    def inner_end():
        for s in range(2):
            for f in (1, 2, 3):
                remote(fwd.at[s, f], fwd.at[s, f], fsend.at[s, f], drecv.at[0], f).wait_send()
            for c in range(PARTS):
                hand(s, 1, c, slot_of(s, 1)).wait_send()
                result(s, c).wait_send()

    def outer_end():
        for s in range(2):
            for f in (2, 3):
                for c in range(PARTS):
                    hand(s, f, c, slot_of(s, f)).wait_send()

    pl.when(inner == 1)(inner_end)
    pl.when(inner == 0)(outer_end)


def run_relayed(send, state, gate, normed, meta, wgu, wdn, cap, n_seq):
    rows, width = state.shape
    ff = wdn.shape[0]
    part = width // PARTS
    dma = pltpu.SemaphoreType.DMA
    return pl.pallas_call(
        functools.partial(relay_kernel, cap, n_seq),
        out_shape=jax.ShapeDtypeStruct((rows, width), BF16),
        in_specs=[ANY, VMEM, VMEM, ANY, VMEM, ANY, ANY],
        out_specs=VMEM,
        scratch_shapes=[
            pltpu.VMEM((8 * cap, width), BF16),
            pltpu.VMEM((8 * cap, width), BF16),
            pltpu.VMEM((4 * cap, width), BF16),
            pltpu.VMEM((2, 2, width, ff), BF16),
            pltpu.VMEM((2, ff, width), BF16),
            pltpu.VMEM((rows, width), F32),
            pltpu.VMEM((2, PARTS, rows, part), BF16),
            pltpu.VMEM((2, 8, rows), F32),
            pltpu.VMEM((2, 4, cap, width), BF16),
            pltpu.VMEM((2, 4, cap, width), BF16),
            pltpu.VMEM((2, PARTS, rows, part), BF16),
            pltpu.VMEM((PARTS, rows, part), BF16),
            dma((2,)), dma((2,)), dma((2,)), dma,
            dma((8,)), dma((8,)), dma((8,)), dma((8,)),
            dma((PARTS,)), dma((2, PARTS)), dma, dma((2,)), dma((2, 4)),
            dma((2, 4, PARTS)), dma((2, 4, PARTS)), dma((2, PARTS)), dma((PARTS,)),
        ],
        compiler_params=pltpu.CompilerParams(
            collective_id=2, has_side_effects=True, vmem_limit_bytes=VMEM_LIMIT
        ),
    )(send, state, gate, normed, meta, wgu, wdn)


def on_device(
    n_branch, n_seq, queries, keyvals, residual, read_list, router, expert_ids, w_gate_up, w_down
):
    rows = queries.shape[1]
    experts = router.shape[1]
    top_count = expert_ids.shape[2]
    capacity = 2 * ((3 * rows * top_count + 4 * experts - 1) // (4 * experts))
    cap = (capacity + 15) // 16 * 16
    kv = keyvals.reshape(rows, -1)
    shifts = [
        lax.ppermute(kv, "seq", [(i, (i + step) % n_seq) for i in range(n_seq)])
        for step in range(1, n_seq)
    ]
    own = jnp.stack([kv] + shifts)
    wgu = jnp.swapaxes(w_gate_up[0], 0, 1)
    line = n_branch == 4 and n_seq == 4 and experts == 8 and top_count == 2
    near = 4 if line else experts
    send, state, gate, normed, meta = attend(
        read_list.reshape(-1), queries[0], own, residual[0], router.T, expert_ids[0],
        experts, near, cap, n_branch, n_seq,
    )
    if line:
        return run_relayed(send, state, gate, normed, meta, wgu, w_down[0], cap, n_seq)[None]
    return run_experts(send, state, gate, wgu, w_down[0], experts, cap, n_seq)[None]


def solution(mesh):
    return jax.shard_map(
        functools.partial(on_device, mesh.shape["branch"], mesh.shape["seq"]),
        mesh=mesh,
        in_specs=(
            P(("rollout", "branch"), "seq", None),
            P(("rollout", "branch"), "seq", None, None),
            P(("rollout", "branch"), "seq", None),
            P(("rollout", "branch"), "seq", None),
            P(),
            P(("rollout", "branch"), "seq", None),
            P(("branch", "seq"), None, None, None),
            P(("branch", "seq"), None, None),
        ),
        out_specs=P(("rollout", "branch"), "seq", None),
        check_vma=False,
    )
```

```python
import functools
import math

import jax
import jax.numpy as jnp
from jax import lax
from jax.experimental import pallas as pl
from jax.experimental.pallas import tpu as pltpu
from jax.sharding import PartitionSpec as P

HEAD_SIZE = 128
PARTS = 4
VMEM_LIMIT = 60 * 1024 * 1024
F32 = jnp.float32
BF16 = jnp.bfloat16
ANY = pl.BlockSpec(memory_space=pl.ANY)
VMEM = pl.BlockSpec(memory_space=pltpu.VMEM)
SMEM = pl.BlockSpec(memory_space=pltpu.SMEM)


def flipped(number, mask, count):
    value, bit = 0, 1
    while bit < count:
        value = value + ((number // bit + mask // bit) % 2) * bit
        bit *= 2
    return value


def attend_kernel(
    experts, cap, n_branch, n_seq,
    list_ref, q_ref, own_ref, res_ref, router_ref, ids_ref, idt_ref,
    send_ref, state_ref, gate_ref, norm_ref, meta_ref,
    picked, sib_ref, tops, totals, ssem, rsem,
):
    branch = lax.axis_index("branch")
    seq = lax.axis_index("seq")
    me = (branch * n_seq + seq) // 2
    rows, width = q_ref.shape
    kv_heads = own_ref.shape[2] // (2 * HEAD_SIZE)
    group = width // HEAD_SIZE // kv_heads
    together = 2
    tall = together * rows
    own_len = n_seq * rows
    sib_len = (n_branch - 1) * rows
    scale = 1.0 / math.sqrt(HEAD_SIZE)
    nt = (((1,), (1,)), ((), ()))

    barrier = pltpu.get_barrier_semaphore()
    for step in range(1, n_branch):
        pl.semaphore_signal(
            barrier, inc=1, device_id={"branch": (branch + step) % n_branch},
            device_id_type=pl.DeviceIdType.MESH,
        )
    for offset in range(n_branch - 1):
        picked[offset] = own_ref[(seq - list_ref[offset] + n_seq) % n_seq]
    pl.semaphore_wait(barrier, n_branch - 1)
    copies = []
    for offset in range(n_branch - 1):
        copy = pltpu.make_async_remote_copy(
            src_ref=picked.at[offset], dst_ref=sib_ref.at[offset],
            send_sem=ssem.at[offset], recv_sem=rsem.at[offset],
            device_id={"branch": (branch + offset + 1) % n_branch},
            device_id_type=pl.DeviceIdType.MESH,
        )
        copy.start()
        copies.append(copy)

    at_row = lax.broadcasted_iota(jnp.int32, (tall, own_len), 0) % rows
    at_col = lax.broadcasted_iota(jnp.int32, (tall, own_len), 1)
    earlier = at_col // rows
    bias = jnp.where(
        earlier == 0,
        jnp.where(at_col <= at_row, 0.0, -1e30),
        jnp.where(earlier <= seq, 0.0, -1e30),
    )

    def head_parts(head, step):
        base = (head * group + step * together) * HEAD_SIZE
        cols = [
            pl.ds(pl.multiple_of(base + i * HEAD_SIZE, HEAD_SIZE), HEAD_SIZE)
            for i in range(together)
        ]
        return cols, jnp.concatenate([q_ref[:, c] for c in cols], axis=0)

    def kv_cols(head):
        return (
            slice(head * HEAD_SIZE, (head + 1) * HEAD_SIZE),
            slice((kv_heads + head) * HEAD_SIZE, (kv_heads + head + 1) * HEAD_SIZE),
        )

    steps = group // together
    for head in range(kv_heads):
        kcol, vcol = kv_cols(head)

        @pl.loop(0, steps)
        def _(step):
            cols, q = head_parts(head, step)
            keys = own_ref[:, :, kcol].reshape(own_len, HEAD_SIZE)
            values = own_ref[:, :, vcol].reshape(own_len, HEAD_SIZE)
            scores = lax.dot_general(q, keys, nt, preferred_element_type=F32) * scale + bias
            top = jnp.max(scores, axis=1, keepdims=True)
            p = jnp.exp(scores - top)
            tops[head * steps + step] = top
            totals[head * steps + step] = jnp.sum(p, axis=1, keepdims=True)
            mixed = jnp.dot(p.astype(BF16), values, preferred_element_type=F32)
            for i, c in enumerate(cols):
                state_ref[:, c] = mixed[i * rows : (i + 1) * rows]

    for copy in copies:
        copy.wait()
    for head in range(kv_heads):
        kcol, vcol = kv_cols(head)

        @pl.loop(0, steps)
        def _(step):
            cols, q = head_parts(head, step)
            keys = sib_ref[:, :, kcol].reshape(sib_len, HEAD_SIZE)
            values = sib_ref[:, :, vcol].reshape(sib_len, HEAD_SIZE)
            scores = lax.dot_general(q, keys, nt, preferred_element_type=F32) * scale
            own_top = tops[head * steps + step]
            top = jnp.maximum(own_top, jnp.max(scores, axis=1, keepdims=True))
            p = jnp.exp(scores - top)
            shrink = jnp.exp(own_top - top)
            total = totals[head * steps + step] * shrink + jnp.sum(p, axis=1, keepdims=True)
            mixed = jnp.dot(p.astype(BF16), values, preferred_element_type=F32)
            inverse = 1.0 / total
            for i, c in enumerate(cols):
                part = slice(i * rows, (i + 1) * rows)
                context = (state_ref[:, c] * shrink[part] + mixed[part]) * inverse[part]
                state_ref[:, c] = res_ref[:, c].astype(F32) + context.astype(BF16).astype(F32)

    state = state_ref[...]
    normed = (
        state * lax.rsqrt(jnp.mean(state * state, axis=1, keepdims=True) + 1e-06)
    ).astype(BF16)
    logits = lax.dot_general(normed, router_ref[...], nt, preferred_element_type=F32)

    top_count = ids_ref.shape[1]
    ids, idt = ids_ref[...], idt_ref[...]
    kinds = lax.broadcasted_iota(jnp.int32, (rows, experts), 1)
    kinds_t = lax.broadcasted_iota(jnp.int32, (experts, rows), 0)
    hot = [(ids[:, k : k + 1] == kinds).astype(F32) for k in range(top_count)]
    hot_t = [(idt[k : k + 1, :] == kinds_t).astype(F32) for k in range(top_count)]
    down = lax.broadcasted_iota(jnp.int32, (rows, rows), 0)
    along = lax.broadcasted_iota(jnp.int32, (rows, rows), 1)
    before = jnp.dot((along < down).astype(F32).astype(BF16), sum(hot).astype(BF16), preferred_element_type=F32)
    before_t = jnp.dot(sum(hot_t).astype(BF16), (down < along).astype(F32).astype(BF16), preferred_element_type=F32)
    dest, dest_t = [], []
    for k in range(top_count):
        slot = jnp.sum(before * hot[k], axis=1, keepdims=True).astype(jnp.int32)
        dest.append((ids[:, k : k + 1] ^ me) * cap + slot)
        slot_t = jnp.sum(before_t * hot_t[k], axis=0, keepdims=True).astype(jnp.int32)
        dest_t.append((idt[k : k + 1, :] ^ me) * cap + slot_t)
    chosen = [jnp.sum(logits * hot[k], axis=1, keepdims=True) for k in range(top_count)]
    gates = [1.0 / sum(jnp.exp(c - chosen[k]) for c in chosen) for k in range(top_count)]

    parts, _, part_width = norm_ref.shape
    for c in range(parts):
        norm_ref[c] = normed[:, c * part_width : (c + 1) * part_width]
    logits_t = lax.dot_general(router_ref[...], normed, nt, preferred_element_type=F32)
    chosen_t = [jnp.sum(logits_t * hot_t[k], axis=0, keepdims=True) for k in range(top_count)]
    meta_ref[...] = jnp.zeros_like(meta_ref)
    for k in range(top_count):
        meta_ref[k : k + 1, :] = dest_t[k].astype(F32)
        meta_ref[top_count + k : top_count + k + 1, :] = 1.0 / sum(
            jnp.exp(c - chosen_t[k]) for c in chosen_t
        )

    pair = 2 * cap
    places = lax.broadcasted_iota(jnp.int32, (rows, pair), 1)
    places_t = lax.broadcasted_iota(jnp.int32, (pair, rows), 0)
    for p in range(send_ref.shape[0] // pair):
        pick = sum((dest_t[k] - p * pair == places_t).astype(F32) for k in range(top_count))
        send_ref[p * pair : (p + 1) * pair, :] = jnp.dot(
            pick.astype(BF16), normed, preferred_element_type=F32
        ).astype(BF16)
        weight = sum(
            jnp.where(dest[k] - p * pair == places, gates[k], 0.0) for k in range(top_count)
        )
        high = weight.astype(BF16)
        gate_ref[p, 0] = high
        gate_ref[p, 1] = (weight - high.astype(F32)).astype(BF16)


def attend(listed, q, own, residual, router_t, ids, experts, near, cap, n_branch, n_seq):
    rows, width = q.shape
    halves = width // HEAD_SIZE // 2
    return pl.pallas_call(
        functools.partial(attend_kernel, experts, cap, n_branch, n_seq),
        out_shape=(
            jax.ShapeDtypeStruct((near * cap, width), BF16),
            jax.ShapeDtypeStruct((rows, width), F32),
            jax.ShapeDtypeStruct((near // 2, 2, rows, 2 * cap), BF16),
            jax.ShapeDtypeStruct((PARTS, rows, width // PARTS), BF16),
            jax.ShapeDtypeStruct((8, rows), F32),
        ),
        in_specs=[SMEM] + [VMEM] * 6,
        out_specs=(VMEM,) * 5,
        scratch_shapes=[
            pltpu.VMEM((n_branch - 1, rows, own.shape[2]), BF16),
            pltpu.VMEM((n_branch - 1, rows, own.shape[2]), BF16),
            pltpu.VMEM((halves, 2 * rows, 1), F32),
            pltpu.VMEM((halves, 2 * rows, 1), F32),
            pltpu.SemaphoreType.DMA((n_branch,)),
            pltpu.SemaphoreType.DMA((n_branch,)),
        ],
        compiler_params=pltpu.CompilerParams(
            collective_id=0, has_side_effects=True, vmem_limit_bytes=VMEM_LIMIT
        ),
    )(listed, q, own, residual, router_t, ids, ids.T)


def expert_kernel(
    experts, cap, n_seq,
    send_ref, state_ref, gate_ref, wgu_ref, wdn_ref, out_ref,
    recv, res, ret, wgu, wdn, acc,
    wsend, wrecv, wloc, lsem, dsend, drecv, bsend, brecv,
):
    branch = lax.axis_index("branch")
    seq = lax.axis_index("seq")
    core = seq % 2
    me = (branch * n_seq + seq) // 2
    pair = 2 * cap
    width = send_ref.shape[1]
    twin = {"seq": seq + 1 - 2 * core}
    mesh_id = pl.DeviceIdType.MESH

    def place(k):
        other = flipped(me, k, experts)
        return {"branch": (2 * other) // n_seq, "seq": (2 * other) % n_seq + core}

    barrier = pltpu.get_barrier_semaphore()
    pl.semaphore_signal(barrier, inc=1, device_id=twin, device_id_type=mesh_id)

    @pl.loop(1, experts)
    def _(k):
        pl.semaphore_signal(barrier, inc=1, device_id=place(k), device_id_type=mesh_id)

    pl.semaphore_wait(barrier, experts)

    def block(k):
        return pl.ds(pl.multiple_of(k * cap, 16), cap)

    def dispatch(k):
        return pltpu.make_async_remote_copy(
            src_ref=send_ref.at[block(k)], dst_ref=recv.at[block(k)],
            send_sem=dsend.at[k], recv_sem=drecv.at[k],
            device_id=place(k), device_id_type=mesh_id,
        )

    def give_back(k):
        return pltpu.make_async_remote_copy(
            src_ref=res.at[block(k)], dst_ref=ret.at[block(k)],
            send_sem=bsend.at[k], recv_sem=brecv.at[k],
            device_id=place(k), device_id_type=mesh_id,
        )

    weights = []
    for i, (src, dst) in enumerate(((wgu_ref, wgu), (wdn_ref, wdn))):
        weights.append(
            pltpu.make_async_remote_copy(
                src_ref=src, dst_ref=dst.at[1], send_sem=wsend.at[i], recv_sem=wrecv.at[i],
                device_id=twin, device_id_type=mesh_id,
            )
        )
        weights.append(pltpu.make_async_copy(src, dst.at[0], wloc.at[i]))
    dispatch(1).start()
    mine = pltpu.make_async_copy(send_ref.at[block(0)], recv.at[block(0)], lsem)
    mine.start()

    @pl.loop(experts // 2, experts)
    def _(k):
        dispatch(k).start()

    @pl.loop(2, experts // 2)
    def _(k):
        dispatch(k).start()

    for copy in weights:
        copy.start()
    acc[...] = state_ref[...]
    for copy in weights:
        copy.wait()

    chunk = 512

    def compute(p):
        span = pl.ds(pl.multiple_of(p * pair, 16), pair)
        acts = []
        for h in range(2):
            x = recv[span, :]
            gate = jnp.dot(x, wgu[h, 0], preferred_element_type=F32)
            up = jnp.dot(x, wgu[h, 1], preferred_element_type=F32)
            acts.append((gate / (1.0 + jnp.exp(-gate)) * up).astype(BF16))
        for start in range(0, width, chunk):
            cols = slice(start, start + chunk)
            done = jnp.dot(acts[0], wdn[0, :, cols], preferred_element_type=F32)
            done += jnp.dot(acts[1], wdn[1, :, cols], preferred_element_type=F32)
            res[span, cols] = done.astype(BF16)

    quarter = experts // 4

    def turn(i):
        return jnp.where(i <= quarter, i + quarter - 1, i - quarter)

    mine.wait()
    dispatch(1).wait_recv()
    compute(0)
    give_back(1).start()

    @pl.loop(1, experts // 2)
    def _(i):
        p = turn(i)
        dispatch(2 * p).wait_recv()
        dispatch(2 * p + 1).wait_recv()
        compute(p)
        give_back(2 * p).start()
        give_back(2 * p + 1).start()

    def add(p, rows):
        for start in range(0, width, chunk):
            cols = slice(start, start + chunk)
            block_rows = rows(cols)
            acc[:, cols] += jnp.dot(
                gate_ref[p, 0], block_rows, preferred_element_type=F32
            ) + jnp.dot(gate_ref[p, 1], block_rows, preferred_element_type=F32)

    give_back(1).wait_recv()
    add(0, lambda cols: jnp.concatenate([res[0:cap, cols], ret[cap:pair, cols]], axis=0))

    @pl.loop(1, experts // 2)
    def _(i):
        p = turn(i)
        give_back(2 * p).wait_recv()
        give_back(2 * p + 1).wait_recv()
        span = pl.ds(pl.multiple_of(p * pair, 16), pair)
        add(p, lambda cols: ret[span, cols])

    out_ref[...] = acc[...].astype(BF16)

    @pl.loop(1, experts)
    def _(k):
        dispatch(k).wait_send()
        give_back(k).wait_send()


def run_experts(send, state, gate, wgu, wdn, experts, cap, n_seq):
    rows, width = state.shape
    ff = wdn.shape[0]
    return pl.pallas_call(
        functools.partial(expert_kernel, experts, cap, n_seq),
        out_shape=jax.ShapeDtypeStruct((rows, width), BF16),
        in_specs=[ANY, VMEM, VMEM, ANY, ANY],
        out_specs=VMEM,
        scratch_shapes=[
            pltpu.VMEM((experts * cap, width), BF16),
            pltpu.VMEM((experts * cap, width), BF16),
            pltpu.VMEM((experts * cap, width), BF16),
            pltpu.VMEM((2, 2, width, ff), BF16),
            pltpu.VMEM((2, ff, width), BF16),
            pltpu.VMEM((rows, width), F32),
            pltpu.SemaphoreType.DMA((2,)),
            pltpu.SemaphoreType.DMA((2,)),
            pltpu.SemaphoreType.DMA((2,)),
            pltpu.SemaphoreType.DMA,
            pltpu.SemaphoreType.DMA((experts,)),
            pltpu.SemaphoreType.DMA((experts,)),
            pltpu.SemaphoreType.DMA((experts,)),
            pltpu.SemaphoreType.DMA((experts,)),
        ],
        compiler_params=pltpu.CompilerParams(
            collective_id=1, has_side_effects=True, vmem_limit_bytes=VMEM_LIMIT
        ),
    )(send, state, gate, wgu, wdn)


def relay_kernel(
    cap, n_seq,
    send_ref, state_ref, gate_ref, norm_ref, meta_ref, wgu_ref, wdn_ref, out_ref,
    recv, res, ret, wgu, wdn, acc, xin, xmeta, fwd, rbuf, xout, far,
    wsend, wrecv, wloc, lsem, dsend, drecv, bsend, brecv,
    csend, crecv, msend, mrecv, fsend, rsend, rrecv, osend, orecv,
):
    experts, near = 8, 4
    branch = lax.axis_index("branch")
    seq = lax.axis_index("seq")
    core = seq % 2
    me = (branch * n_seq + seq) // 2
    inner = (branch + 1) // 2 % 2
    pair = 2 * cap
    rows, width = state_ref.shape
    step = width // PARTS
    twin = {"seq": seq + 1 - 2 * core}
    mesh_id = pl.DeviceIdType.MESH

    def place(k):
        other = flipped(me, k, experts)
        return {"branch": (2 * other) // n_seq, "seq": (2 * other) % n_seq + core}

    barrier = pltpu.get_barrier_semaphore()
    pl.semaphore_signal(barrier, inc=1, device_id=twin, device_id_type=mesh_id)
    for k in range(1, experts):
        pl.semaphore_signal(barrier, inc=1, device_id=place(k), device_id_type=mesh_id)
    pl.semaphore_wait(barrier, experts)

    def block(k):
        return pl.ds(pl.multiple_of(k * cap, 16), cap)

    def remote(src, dst, send, arrive, k):
        return pltpu.make_async_remote_copy(
            src_ref=src, dst_ref=dst, send_sem=send, recv_sem=arrive,
            device_id=place(k), device_id_type=mesh_id,
        )

    def dispatch(k):
        return remote(send_ref.at[block(k)], recv.at[block(k)], dsend.at[k], drecv.at[k], k)

    def give_back(k):
        return remote(res.at[block(k)], ret.at[block(k)], bsend.at[k], brecv.at[k], k)

    across = 4 + 2 * inner

    def cross(c):
        return remote(norm_ref.at[c], xin.at[1 - inner, c], csend.at[c], crecv.at[1 - inner, c], across)

    def cross_meta():
        return remote(meta_ref, xmeta.at[1 - inner], msend, mrecv.at[1 - inner], across)

    def arrived(s, c):
        return remote(norm_ref.at[c], xin.at[s, c], csend.at[c], crecv.at[s, c], across)

    def slot_of(s, f):
        return f ^ (6 - 2 * s)

    def part(c):
        return slice(c * step, (c + 1) * step)

    def forward(s, f, c):
        k = slot_of(s, f)
        src = fwd.at[s, f, :, part(c)]
        dst = recv.at[block(k), part(c)]
        if f == 0:
            return pltpu.make_async_copy(src, dst, drecv.at[k])
        return remote(src, dst, fsend.at[s, f], drecv.at[k], f)

    def got(k):
        remote(recv.at[block(k)], recv.at[block(k)], dsend.at[k], drecv.at[k], 1).wait_recv()

    weights = []
    for i, (src, dst) in enumerate(((wgu_ref, wgu), (wdn_ref, wdn))):
        weights.append(
            pltpu.make_async_remote_copy(
                src_ref=src, dst_ref=dst.at[1], send_sem=wsend.at[i], recv_sem=wrecv.at[i],
                device_id=twin, device_id_type=mesh_id,
            )
        )
        weights.append(pltpu.make_async_copy(src, dst.at[0], wloc.at[i]))

    def start_cross():
        cross_meta().start()
        for c in range(PARTS):
            cross(c).start()

    for copy in weights:
        copy.start()
    pl.when(inner == 1)(start_cross)
    mine = pltpu.make_async_copy(send_ref.at[block(0)], recv.at[block(0)], lsem)
    mine.start()
    for k in (1, 2, 3):
        dispatch(k).start()
    pl.when(inner == 0)(start_cross)
    acc[...] = state_ref[...]

    def rows_of(s):
        where = lax.broadcasted_iota(jnp.int32, (cap, rows), 0).astype(F32)
        meta = xmeta[s]
        return meta, [where + float(slot_of(s, f) * cap) for f in range(near)]

    def relay(s):
        remote(meta_ref, xmeta.at[s], msend, mrecv.at[s], across).wait_recv()
        meta, where = rows_of(s)
        pick = jnp.concatenate(
            [(meta[0:1] == w).astype(F32) + (meta[1:2] == w).astype(F32) for w in where], axis=0
        ).astype(BF16)
        for c in range(PARTS):
            arrived(s, c).wait_recv()
            taken = jnp.dot(pick, xin[s, c], preferred_element_type=F32).astype(BF16)
            for f in range(near):
                fwd[s, f, :, part(c)] = taken[f * cap : (f + 1) * cap]
            for f in (2, 3, 1, 0):
                forward(s, f, c).start()

    def hand(s, f, c, k):
        src = res.at[block(k), part(c)]
        dst = rbuf.at[s, f, :, part(c)]
        if f == 0:
            return pltpu.make_async_copy(src, dst, rrecv.at[s, f, c])
        return remote(src, dst, rsend.at[s, f, c], rrecv.at[s, f, c], f)

    def compute(p, after=None):
        span = pl.ds(pl.multiple_of(p * pair, 16), pair)
        acts = []
        for h in range(2):
            x = recv[span, :]
            gate = jnp.dot(x, wgu[h, 0], preferred_element_type=F32)
            up = jnp.dot(x, wgu[h, 1], preferred_element_type=F32)
            acts.append((gate / (1.0 + jnp.exp(-gate)) * up).astype(BF16))
        for c in range(PARTS):
            done = jnp.dot(acts[0], wdn[0, :, part(c)], preferred_element_type=F32)
            done += jnp.dot(acts[1], wdn[1, :, part(c)], preferred_element_type=F32)
            res[span, part(c)] = done.astype(BF16)
            if after is not None:
                after(c)

    pl.when(inner == 1)(lambda: relay(0))
    for copy in weights:
        copy.wait()
    mine.wait()
    got(1)
    compute(0)
    give_back(1).start()
    pl.when(inner == 1)(lambda: relay(1))

    def far_group(s, base):
        def after(c):
            for f in (base, base + 1):
                hand(s, f, c, slot_of(s, f)).start()

        k = slot_of(s, base) // 2 * 2
        got(k)
        got(k + 1)
        compute(k // 2, after)

    for s in range(2):
        pl.when(inner == 1)(functools.partial(far_group, s, 0))
        pl.when(inner == 0)(functools.partial(far_group, s, 2))

    def result(s, c):
        return remote(xout.at[s, c], far.at[c], osend.at[s, c], orecv.at[c], 6 - 2 * s)

    def combine(s):
        meta, where = rows_of(s)
        weight = jnp.concatenate(
            [
                jnp.where(meta[0:1] == w, meta[2:3], 0.0) + jnp.where(meta[1:2] == w, meta[3:4], 0.0)
                for w in where
            ],
            axis=0,
        ).T
        high = weight.astype(BF16)
        low = (weight - high.astype(F32)).astype(BF16)
        for c in range(PARTS):
            for f in range(near):
                if f == 0:
                    hand(s, 0, c, slot_of(s, 0)).wait()
                else:
                    hand(s, f, c, slot_of(s, f)).wait_recv()
            given = rbuf[s, :, :, part(c)].reshape(near * cap, step)
            xout[s, c] = (
                jnp.dot(high, given, preferred_element_type=F32)
                + jnp.dot(low, given, preferred_element_type=F32)
            ).astype(BF16)
            result(s, c).start()

    pl.when(inner == 1)(lambda: combine(0))
    got(2)
    got(3)
    compute(1)
    give_back(2).start()
    give_back(3).start()
    pl.when(inner == 1)(lambda: combine(1))

    for p in range(near // 2):
        for k in (2 * p, 2 * p + 1):
            if k:
                give_back(k).wait_recv()
        for c in range(PARTS):
            cols = part(c)
            low = res if p == 0 else ret
            given = jnp.concatenate(
                [low[2 * p * cap : (2 * p + 1) * cap, cols], ret[(2 * p + 1) * cap : (2 * p + 2) * cap, cols]],
                axis=0,
            )
            acc[:, cols] += jnp.dot(gate_ref[p, 0], given, preferred_element_type=F32) + jnp.dot(
                gate_ref[p, 1], given, preferred_element_type=F32
            )
    for c in range(PARTS):
        result(0, c).wait_recv()
        out_ref[:, part(c)] = (acc[:, part(c)] + far[c].astype(F32)).astype(BF16)

    for k in (1, 2, 3):
        dispatch(k).wait_send()
        give_back(k).wait_send()
    cross_meta().wait_send()
    for c in range(PARTS):
        cross(c).wait_send()

    def inner_end():
        for s in range(2):
            for f in (1, 2, 3):
                remote(fwd.at[s, f], fwd.at[s, f], fsend.at[s, f], drecv.at[0], f).wait_send()
            for c in range(PARTS):
                hand(s, 1, c, slot_of(s, 1)).wait_send()
                result(s, c).wait_send()

    def outer_end():
        for s in range(2):
            for f in (2, 3):
                for c in range(PARTS):
                    hand(s, f, c, slot_of(s, f)).wait_send()

    pl.when(inner == 1)(inner_end)
    pl.when(inner == 0)(outer_end)


def run_relayed(send, state, gate, normed, meta, wgu, wdn, cap, n_seq):
    rows, width = state.shape
    ff = wdn.shape[0]
    part = width // PARTS
    dma = pltpu.SemaphoreType.DMA
    return pl.pallas_call(
        functools.partial(relay_kernel, cap, n_seq),
        out_shape=jax.ShapeDtypeStruct((rows, width), BF16),
        in_specs=[ANY, VMEM, VMEM, ANY, VMEM, ANY, ANY],
        out_specs=VMEM,
        scratch_shapes=[
            pltpu.VMEM((8 * cap, width), BF16),
            pltpu.VMEM((8 * cap, width), BF16),
            pltpu.VMEM((4 * cap, width), BF16),
            pltpu.VMEM((2, 2, width, ff), BF16),
            pltpu.VMEM((2, ff, width), BF16),
            pltpu.VMEM((rows, width), F32),
            pltpu.VMEM((2, PARTS, rows, part), BF16),
            pltpu.VMEM((2, 8, rows), F32),
            pltpu.VMEM((2, 4, cap, width), BF16),
            pltpu.VMEM((2, 4, cap, width), BF16),
            pltpu.VMEM((2, PARTS, rows, part), BF16),
            pltpu.VMEM((PARTS, rows, part), BF16),
            dma((2,)), dma((2,)), dma((2,)), dma,
            dma((8,)), dma((8,)), dma((8,)), dma((8,)),
            dma((PARTS,)), dma((2, PARTS)), dma, dma((2,)), dma((2, 4)),
            dma((2, 4, PARTS)), dma((2, 4, PARTS)), dma((2, PARTS)), dma((PARTS,)),
        ],
        compiler_params=pltpu.CompilerParams(
            collective_id=2, has_side_effects=True, vmem_limit_bytes=VMEM_LIMIT
        ),
    )(send, state, gate, normed, meta, wgu, wdn)


def on_device(
    n_branch, n_seq, queries, keyvals, residual, read_list, router, expert_ids, w_gate_up, w_down
):
    rows = queries.shape[1]
    experts = router.shape[1]
    top_count = expert_ids.shape[2]
    capacity = 2 * ((3 * rows * top_count + 4 * experts - 1) // (4 * experts))
    cap = (capacity + 15) // 16 * 16
    kv = keyvals.reshape(rows, -1)
    shifts = [
        lax.ppermute(kv, "seq", [(i, (i + step) % n_seq) for i in range(n_seq)])
        for step in range(1, n_seq)
    ]
    own = jnp.stack([kv] + shifts)
    wgu = jnp.swapaxes(w_gate_up[0], 0, 1)
    line = n_branch == 4 and n_seq == 4 and experts == 8 and top_count == 2
    near = 4 if line else experts
    send, state, gate, normed, meta = attend(
        read_list.reshape(-1), queries[0], own, residual[0], router.T, expert_ids[0],
        experts, near, cap, n_branch, n_seq,
    )
    if line:
        return run_relayed(send, state, gate, normed, meta, wgu, w_down[0], cap, n_seq)[None]
    return run_experts(send, state, gate, wgu, w_down[0], experts, cap, n_seq)[None]


def solution(mesh):
    return jax.shard_map(
        functools.partial(on_device, mesh.shape["branch"], mesh.shape["seq"]),
        mesh=mesh,
        in_specs=(
            P(("rollout", "branch"), "seq", None),
            P(("rollout", "branch"), "seq", None, None),
            P(("rollout", "branch"), "seq", None),
            P(("rollout", "branch"), "seq", None),
            P(),
            P(("rollout", "branch"), "seq", None),
            P(("branch", "seq"), None, None, None),
            P(("branch", "seq"), None, None),
        ),
        out_specs=P(("rollout", "branch"), "seq", None),
        check_vma=False,
    )
```
